128 devices in a mesh: frame: 16 (over x, z), head: 8 (over y, core).
Axes of the slice: x: 4, y: 4, z: 4, core: 2. Of those that a mesh axis runs over, the one named last changes fastest.
Arguments:
- queries: bfloat16 [8192, 1024], P('frame', 'head'), may hold values from -6 to 6
- keys: bfloat16 [8192, 1024], P('frame', 'head'), may hold values from -6 to 6
- values: bfloat16 [8192, 1024], P('frame', 'head'), may hold values from -6 to 6
- band_width: int32 [16, 8], replicated, may hold values from 1 to 4, as said below
- band_offset: int32 [16, 8, 4], replicated, may hold values from 0 to 3
- out_weight: bfloat16 [1024, 1536], P('head'), may hold values from -0.1875 to 0.1875
Outputs:
- projected: bfloat16 [8192, 1536], P(('frame', 'head'))
The draws below stay inside these ranges and needn't reach their ends.
Inputs may be any that keep to these rules, and one draw needn't show every extreme that they name: `band_width`: for distances 0 and 1 the widths lie in (2, 4], for 2 and 3 in (1, 2], for 4 to 7 in [1, 1]; each of these upper ends is reached by some frame.
All inputs are finite; a program needn't handle non-finite values.
Results may differ from the reference program's by a relative error of at most 0.015.
Values may be sent and summed in bfloat16 or wider, within the bound.
A program may use at most 64 MiB of HBM per device.

```python
import math
import jax
import jax.numpy as jnp
from jax import lax

D = 1536
HEADS = 8
HEAD = 128
TF = 512
BLK = 128
RADIUS = 7
FRAMES = 16
NB = 4
TOKENS = 8192


def paired_draw(key):
    keys_raw = jnp.clip(jax.random.normal(jax.random.fold_in(key, 11), (TOKENS, HEADS * HEAD), jnp.float32), -6.0, 6.0)
    query_raw = jnp.clip(jax.random.normal(jax.random.fold_in(key, 12), (TOKENS, HEADS * HEAD), jnp.float32), -6.0, 6.0)
    return (query_raw, keys_raw)


def draw_queries(key, part):
    query_raw, keys_raw = paired_draw(key)
    return query_raw.astype(jnp.bfloat16)


def draw_keys(key, part):
    query_raw, keys_raw = paired_draw(key)
    return keys_raw.astype(jnp.bfloat16)


def draw_band_width(key, part):
    column = jnp.arange(RADIUS + 1)
    upper = jnp.where(column <= 1, NB, jnp.where(column <= 3, NB // 2, NB // 4))
    lower = jnp.where(column <= 1, NB // 2 + 1, jnp.where(column <= 3, NB // 4 + 1, 1))
    raw = jax.random.randint(jax.random.fold_in(key, 21), (FRAMES, RADIUS + 1), 0, 1 << 20)
    widths = lower[None, :] + raw % (upper - lower + 1)[None, :]
    chosen = jax.random.randint(jax.random.fold_in(key, 22), (), 0, FRAMES)
    widths = jnp.where(jnp.arange(FRAMES)[:, None] == chosen, upper[None, :], widths)
    return widths.astype(jnp.int32)


def draw_band_offset(key, part):
    return jax.random.randint(jax.random.fold_in(key, 31), (FRAMES, RADIUS + 1, NB), 0, NB).astype(jnp.int32)


def levels(own_key, shape, cuts, smallest, top_value):
    loudness = 1.0
    for position, blocks in cuts:
        heights = jax.random.uniform(jax.random.fold_in(jax.random.fold_in(own_key, 6), position), (blocks,), jnp.float32, smallest / len(cuts), top_value / len(cuts))
        loudness = loudness * jnp.repeat(jnp.exp(heights), shape[position] // blocks).reshape((-1,) + (1,) * (len(shape) - 1 - position))
    return loudness


def bell_draw(rng, shape, scale, bound, split=(), kind=jnp.bfloat16):
    array = jax.random.normal(rng, shape, jnp.float32) * scale
    if len(split) > 0:
        array = levels(rng, shape, split, -0.22, 0.18) * array
    return jnp.clip(array, min=-bound, max=bound).astype(kind)


def setup_inputs(seed: int = 0) -> dict:
    splits = jax.random.split(jax.random.key(seed), 7)
    return {
        "queries": draw_queries(jax.random.fold_in(splits[6], 71), 0),
        "keys": draw_keys(jax.random.fold_in(splits[6], 71), 0),
        "values": bell_draw(splits[2], (TOKENS, HEADS * HEAD), 1.0, 6.0, ((0, 16), (1, 8))),
        "band_width": draw_band_width(jax.random.fold_in(splits[6], 71), 0),
        "band_offset": draw_band_offset(jax.random.fold_in(splits[6], 71), 0),
        "out_weight": bell_draw(splits[5], (HEADS * HEAD, D), (HEADS * HEAD) ** -0.5, 0.1875, ((0, 8),)),
    }


def block_mask(this_frame, key_frame, frames, band_width, band_offset, block_count):
    distance = jnp.abs(key_frame - this_frame)
    present = (key_frame >= 0) & (key_frame < frames) & (distance <= RADIUS)
    reach = jnp.minimum(distance, RADIUS)
    band_span = band_width[this_frame, reach]
    offsets = band_offset[this_frame, reach]
    query_block = lax.broadcasted_iota(jnp.int32, (block_count, block_count), 0)
    key_block = lax.broadcasted_iota(jnp.int32, (block_count, block_count), 1)
    inside = jnp.mod(key_block - offsets[:, None], block_count) < band_span
    diagonal = (reach == 0) & (query_block == key_block)
    return present & (inside | diagonal)

def reference(queries, keys, values, band_width, band_offset, out_weight):
    score_scale = 1.0 / math.sqrt(HEAD)

    def attend_pair(pair):
        this_frame = (pair // HEADS).astype(jnp.int32)
        head_index = (pair % HEADS).astype(jnp.int32)
        column = (head_index * HEAD).astype(jnp.int32)
        query_rows = lax.dynamic_slice(queries, ((this_frame * TF).astype(jnp.int32), column), (TF, HEAD))
        key_list = []
        value_list = []
        mask_list = []
        for shift_step in range(-RADIUS, RADIUS + 1):
            key_frame = this_frame + shift_step
            clipped = jnp.clip(key_frame, 0, FRAMES - 1).astype(jnp.int32)
            start_row = (clipped * TF).astype(jnp.int32)
            key_list.append(lax.dynamic_slice(keys, (start_row, column), (TF, HEAD)))
            value_list.append(lax.dynamic_slice(values, (start_row, column), (TF, HEAD)))
            blocks = block_mask(this_frame, key_frame, FRAMES, band_width, band_offset, NB)
            mask_list.append(jnp.repeat(jnp.repeat(blocks, BLK, axis=0), BLK, axis=1))
        key_all = jnp.concatenate(key_list, axis=0)
        value_all = jnp.concatenate(value_list, axis=0)
        mask_all = jnp.concatenate(mask_list, axis=1)
        scores = jnp.dot(query_rows, key_all.T, preferred_element_type=jnp.float32) * score_scale
        scores = jnp.where(mask_all, scores, -1e+30)
        peak = lax.optimization_barrier(jnp.max(scores, axis=1, keepdims=True))
        weights = jnp.where(mask_all, jnp.exp(scores - peak), 0.0)
        totals = lax.optimization_barrier(jnp.sum(weights, axis=1, keepdims=True))
        mixed = jnp.dot(weights.astype(jnp.bfloat16), value_all, preferred_element_type=jnp.float32)
        return mixed / totals
    pairs = jnp.arange(FRAMES * HEADS, dtype=jnp.int32)
    heads_out = lax.map(attend_pair, pairs)
    attended = heads_out.reshape(FRAMES, HEADS, TF, HEAD).transpose(0, 2, 1, 3)
    attended = attended.reshape(TOKENS, HEADS * HEAD).astype(jnp.bfloat16)
    return jnp.dot(attended, out_weight, preferred_element_type=jnp.float32).astype(jnp.bfloat16)
```

```python
import functools
import math

import jax
import jax.numpy as jnp
from jax import lax
from jax.experimental import pallas as pl
from jax.experimental.pallas import tpu as pltpu
from jax.sharding import PartitionSpec as P

RING = 4
HEADS = 8
HEAD = 128
BLK = 128
NB = 4
RADIUS = 7
ROWS = 64
PACKED = ROWS + 16
EXPONENT = math.log2(math.e) / math.sqrt(HEAD)
MESH = pl.DeviceIdType.MESH
BF16, F32 = jnp.bfloat16, jnp.float32


def turn(value, steps):
    return lax.rem(value + (RING + steps), RING)


def kernel(
    width_ref, offset_ref, q_hbm, k_hbm, v_hbm, w_hbm, out_ref,
    k_0, k_1, k_2, k_3, v_0, v_1, v_2, v_3, q_all, w_all,
    peak_ref, total_ref, mixed_ref, packed, arrived, attended,
    local_sem, kv_send, kv_recv, q_send, q_recv, w_send, w_recv, o_send, o_recv, self_sem,
):
    frame, head = lax.axis_index("frame"), lax.axis_index("head")
    x, z = lax.div(frame, RING), lax.rem(frame, RING)
    y, core = lax.div(head, 2), lax.rem(head, 2)

    def at(x, z, head):
        return (x * RING + z, head)

    x_next, x_last = at(turn(x, 1), z, head), at(turn(x, -1), z, head)
    z_next, z_last = at(x, turn(z, 1), head), at(x, turn(z, -1), head)
    head_next, head_last = turn(y, 1) * 2 + core, turn(y, -1) * 2 + core
    head_far, head_pair = turn(y, 2) * 2 + core, y * 2 + 1 - core
    y_next, y_last, pair = at(x, z, head_next), at(x, z, head_last), at(x, z, head_pair)

    def remote(source, target, send, recv, device):
        return pltpu.make_async_remote_copy(
            src_ref=source, dst_ref=target, send_sem=send, recv_sem=recv,
            device_id=device, device_id_type=MESH,
        )

    own = [
        pltpu.make_async_copy(q_hbm, q_all.at[0], local_sem.at[0]),
        pltpu.make_async_copy(k_hbm, k_0, local_sem.at[1]),
        pltpu.make_async_copy(v_hbm, v_0, local_sem.at[2]),
        pltpu.make_async_copy(w_hbm, w_all.at[head], local_sem.at[3]),
    ]
    for copy in own:
        copy.start()

    barrier = pltpu.get_barrier_semaphore()
    for device in (x_next, x_last):
        pl.semaphore_signal(barrier, inc=1, device_id=device, device_id_type=MESH)

    def greet(step, carry):
        other_z, other_head = lax.div(step, HEADS), lax.rem(step, HEADS)

        @pl.when((other_z != z) | (other_head != head))
        def _():
            pl.semaphore_signal(
                barrier, inc=1, device_id=at(x, other_z, other_head), device_id_type=MESH
            )

        return carry

    lax.fori_loop(0, RING * HEADS, greet, 0)
    pl.semaphore_wait(barrier, RING * HEADS + 1)

    kv = [
        remote(k_hbm, k_1, kv_send.at[0], kv_recv.at[0], x_next),
        remote(v_hbm, v_3, kv_send.at[1], kv_recv.at[1], x_last),
        remote(v_hbm, v_1, kv_send.at[2], kv_recv.at[2], x_next),
        remote(k_hbm, k_3, kv_send.at[3], kv_recv.at[3], x_last),
        remote(k_1, k_2, kv_send.at[4], kv_recv.at[4], x_next),
        remote(v_3, v_2, kv_send.at[5], kv_recv.at[5], x_last),
    ]
    low, high = pl.ds(0, NB // 2), pl.ds(NB // 2, NB // 2)
    qs = [
        remote(q_hbm.at[low], q_all.at[1, low], q_send.at[0], q_recv.at[0], z_next),
        remote(q_hbm.at[high], q_all.at[3, high], q_send.at[1], q_recv.at[1], z_last),
        remote(q_hbm.at[high], q_all.at[1, high], q_send.at[2], q_recv.at[2], z_next),
        remote(q_hbm.at[low], q_all.at[3, low], q_send.at[3], q_recv.at[3], z_last),
        remote(q_all.at[1, low], q_all.at[2, low], q_send.at[4], q_recv.at[4], z_next),
        remote(q_all.at[3, high], q_all.at[2, high], q_send.at[5], q_recv.at[5], z_last),
    ]
    top, end = pl.ds(0, HEAD // 2), pl.ds(HEAD // 2, HEAD // 2)
    ws = [
        remote(w_hbm.at[top], w_all.at[head, top], w_send.at[0], w_recv.at[0], y_next),
        remote(w_hbm.at[end], w_all.at[head, end], w_send.at[1], w_recv.at[1], y_last),
        remote(w_hbm.at[end], w_all.at[head, end], w_send.at[2], w_recv.at[2], y_next),
        remote(w_hbm.at[top], w_all.at[head, top], w_send.at[3], w_recv.at[3], y_last),
        remote(w_all.at[head_last, top], w_all.at[head_last, top], w_send.at[4], w_recv.at[4], y_next),
        remote(w_all.at[head_next, end], w_all.at[head_next, end], w_send.at[5], w_recv.at[5], y_last),
        remote(w_hbm, w_all.at[head], w_send.at[6], w_recv.at[6], pair),
        remote(w_all.at[head_last], w_all.at[head_last], w_send.at[7], w_recv.at[7], pair),
        remote(w_all.at[head_next], w_all.at[head_next], w_send.at[8], w_recv.at[8], pair),
        remote(w_all.at[head_far], w_all.at[head_far], w_send.at[9], w_recv.at[9], pair),
    ]
    for step in range(4):
        qs[step].start()
        kv[step].start()
    for step in range(4):
        ws[step].start()
    ws[6].start()

    ones = jnp.ones((BLK, HEAD), BF16)

    def query_frame(slot):
        return x * RING + turn(z, -slot)

    def gap(slot, key_frame):
        this = query_frame(slot)
        return jnp.maximum(this - key_frame, key_frame - this)

    def absorb(first, slot, block, scores, value_rows):
        rows = pl.ds(block * BLK, BLK)
        peak = jnp.max(functools.reduce(jnp.maximum, scores), axis=1, keepdims=True)
        if not first:
            before = peak_ref[slot, rows, :]
            peak = jnp.maximum(before, peak)
            keep = jnp.exp2((before - peak) * EXPONENT)
        weights = [jnp.exp2((part - peak) * EXPONENT).astype(BF16) for part in scores]
        weights = jnp.concatenate(weights, axis=1) if len(weights) > 1 else weights[0]
        extended = jnp.concatenate(
            [value_rows, jnp.concatenate([ones] * len(scores), axis=0)], axis=1
        )
        update = jnp.dot(weights, extended, preferred_element_type=F32)
        mixed, total = update[:, :HEAD], update[:, HEAD:]
        if not first:
            mixed += mixed_ref[slot, rows, :] * keep
            total += total_ref[slot, rows, :] * keep
        peak_ref[slot, rows, :] = jnp.broadcast_to(peak, (BLK, HEAD))
        mixed_ref[slot, rows, :] = mixed
        total_ref[slot, rows, :] = total

    def times(query_rows, key_rows):
        return lax.dot_general(
            query_rows, key_rows, (((1,), (1,)), ((), ())), preferred_element_type=F32
        )

    def query_rows(slot, block):
        return q_all[slot, block]

    def wide(first, slot, distance, k_ref, v_ref):
        this = query_frame(slot)
        span = width_ref[distance, this]
        tokens = NB * BLK
        keys, values = k_ref[...].reshape(tokens, HEAD), v_ref[...].reshape(tokens, HEAD)
        key_block = lax.broadcasted_iota(jnp.int32, (1, tokens), 1) // BLK
        for block in range(NB):
            scores = times(query_rows(slot, block), keys)
            past = lax.rem(key_block + (NB - offset_ref[distance, block, this]), NB)
            diagonal = key_block == jnp.where(distance == 0, block, NB)
            scores += jnp.where((past < span) | diagonal, 0.0, -1e30)
            parts = [scores[:, other * BLK:(other + 1) * BLK] for other in range(NB)]
            absorb(first, slot, block, parts, values)

    def narrow(first, slot, distance, k_ref, v_ref, count):
        this = query_frame(slot)
        for block in range(NB):
            offset = offset_ref[distance, block, this]
            keys, values = [], []
            for step in range(count):
                chosen = lax.rem(offset + step, NB)
                keys.append(k_ref[chosen])
                values.append(v_ref[chosen])
            if count > 1:
                keys, values = [jnp.concatenate(keys, axis=0)], [jnp.concatenate(values, axis=0)]
            scores = times(query_rows(slot, block), keys[0])
            parts = [scores[:, step * BLK:(step + 1) * BLK] for step in range(count)]
            absorb(first, slot, block, parts, values[0])

    def take(first, slot, key_frame, k_ref, v_ref, singles):
        distance = gap(slot, key_frame)

        @pl.when(distance <= 1)
        def _():
            wide(first, slot, distance, k_ref, v_ref)

        @pl.when((distance >= 2) & (distance <= 3))
        def _():
            narrow(first, slot, distance, k_ref, v_ref, 2)

        if singles:

            @pl.when((distance >= 4) & (distance <= RADIUS))
            def _():
                narrow(first, slot, distance, k_ref, v_ref, 1)

    qs[0].wait_recv()
    qs[4].start()
    qs[1].wait_recv()
    qs[5].start()
    for copy in own[:3]:
        copy.wait()
    kv[0].wait_recv()
    kv[4].start()
    kv[1].wait_recv()
    kv[5].start()
    ws[0].wait_recv()
    ws[4].start()
    ws[1].wait_recv()
    ws[5].start()
    for step in range(2, 6):
        qs[step].wait_recv()

    def stage(first, steps, k_ref, v_ref):
        key_frame = turn(x, steps) * RING + z

        def each(slot, carry):
            take(first, slot, key_frame, k_ref, v_ref, not first)
            return carry

        lax.fori_loop(0, RING, each, 0)

    stage(True, 0, k_0, v_0)
    kv[2].wait_recv()
    stage(False, -1, k_1, v_1)
    kv[3].wait_recv()
    stage(False, 1, k_3, v_3)

    ws[2].wait_recv()
    ws[7].start()
    ws[3].wait_recv()
    ws[8].start()

    far_frame = turn(x, 2) * RING + z
    row = lax.broadcasted_iota(jnp.int32, (BLK, BLK), 0)
    lane = lax.broadcasted_iota(jnp.int32, (BLK, BLK), 1)
    small_row = lax.broadcasted_iota(jnp.int32, (16, BLK), 0)

    def share(slot, receiver):
        return packed.at[slot, receiver], arrived.at[head, z]

    def finish(slot):
        for block in range(NB):
            rows = pl.ds(block * BLK, BLK)
            total = total_ref[slot, rows, :]
            scaled = (mixed_ref[slot, rows, :] / total).astype(BF16)
            level = peak_ref[slot, rows, :] * EXPONENT + jnp.log(total) * math.log2(math.e)
            level = jnp.sum(jnp.where(row == lane, level, 0.0), axis=0, keepdims=True)
            high_part = level.astype(BF16).astype(F32)
            rest = level - high_part
            mid_part = rest.astype(BF16).astype(F32)
            tile = jnp.where(
                small_row == 0, high_part,
                jnp.where(small_row == 1, mid_part, jnp.where(small_row == 2, rest - mid_part, 0.0)),
            ).astype(BF16)
            for half in range(2):
                packed[slot, 2 * block + half, 0:ROWS, :] = scaled[half * ROWS:(half + 1) * ROWS]
                packed[slot, 2 * block + half, ROWS:PACKED, :] = tile

        def send(receiver, carry):
            source, target = share(slot, receiver)
            here = (slot == 0) & (receiver == head)

            @pl.when(here)
            def _():
                pltpu.make_async_copy(source, target, self_sem).start()

            @pl.when(jnp.logical_not(here))
            def _():
                remote(
                    source, target, o_send.at[slot], o_recv.at[head], at(x, turn(z, -slot), receiver)
                ).start()

            return carry

        lax.fori_loop(0, HEADS, send, 0)

    def closing(step, carry):
        late, turn_of = lax.div(step, RING), lax.rem(step, RING)
        slot = lax.rem(2 + 3 * turn_of + 3 * lax.div(turn_of, 2) + 2 * lax.div(turn_of, 3), RING)
        distance = gap(slot, far_frame)
        needs = distance <= RADIUS

        @pl.when(step == RING)
        def _():
            kv[4].wait_recv()
            kv[5].wait_recv()

        @pl.when((late == 0) & jnp.logical_not(needs))
        def _():
            finish(slot)

        @pl.when((late == 1) & needs)
        def _():
            narrow(False, slot, distance, k_2, v_2, 1)
            finish(slot)

        return carry

    lax.fori_loop(0, 2 * RING, closing, 0)

    ws[4].wait_recv()
    ws[5].wait_recv()
    ws[9].start()

    pltpu.make_async_copy(packed.at[0, head], arrived.at[head, z], self_sem).wait()
    column = lax.broadcasted_iota(jnp.int32, (ROWS, HEAD), 1)
    here = lax.broadcasted_iota(jnp.int32, (ROWS, HEAD), 0) + core * ROWS
    for other in range(HEADS):
        mine = other == head

        @pl.when(mine)
        def _():
            three = pltpu.make_async_copy(
                arrived.at[other, pl.ds(0, 3)], arrived.at[other, pl.ds(0, 3)], o_recv.at[other]
            )
            three.wait()

        @pl.when(jnp.logical_not(mine))
        def _():
            four = pltpu.make_async_copy(arrived.at[other], arrived.at[other], o_recv.at[other])
            four.wait()

    for other in range(HEADS):
        levels = []
        for part in range(RING):
            tile = arrived[other, part, ROWS:PACKED, :].astype(F32)
            levels.append(jnp.sum(tile, axis=0, keepdims=True))
        peak = functools.reduce(jnp.maximum, levels)
        shares = [jnp.exp2(level - peak) for level in levels]
        whole = functools.reduce(jnp.add, shares)
        merged = jnp.zeros((ROWS, HEAD), F32)
        for part in range(RING):
            share_row = shares[part] / whole
            share_column = jnp.sum(
                jnp.where(column == here, jnp.broadcast_to(share_row, (ROWS, HEAD)), 0.0),
                axis=1, keepdims=True,
            )
            merged += arrived[other, part, 0:ROWS, :].astype(F32) * share_column
        attended[:, other * HEAD:(other + 1) * HEAD] = merged.astype(BF16)

    own[3].wait()
    for step in range(6, 10):
        ws[step].wait_recv()
    depth, columns = HEADS * HEAD, w_all.shape[2]
    tile = 512
    for start in range(0, columns, tile):
        weight = w_all[:, :, start:start + tile].reshape(depth, tile)
        out_ref[:, start:start + tile] = jnp.dot(
            attended[...], weight, preferred_element_type=F32
        ).astype(BF16)

    for copy in kv + qs + ws:
        copy.wait_send()
    seven = packed.at[0, pl.ds(0, HEADS - 1)]
    pltpu.make_async_copy(seven, seven, o_send.at[0]).wait()
    for slot in range(1, RING):
        pltpu.make_async_copy(packed.at[slot], packed.at[slot], o_send.at[slot]).wait()


def on_device(queries, keys, values, band_width, band_offset, out_weight):
    tokens, width = queries.shape[0], out_weight.shape[1]
    queries, keys, values = (array.reshape(NB, BLK, HEAD) for array in (queries, keys, values))
    band_width, band_offset = band_width.T, band_offset.transpose(1, 2, 0)
    block = pltpu.VMEM((NB, BLK, HEAD), BF16)
    state = pltpu.VMEM((RING, tokens, HEAD), F32)
    dma = pltpu.SemaphoreType.DMA
    smem, anywhere = pl.BlockSpec(memory_space=pltpu.SMEM), pl.BlockSpec(memory_space=pltpu.HBM)
    return pl.pallas_call(
        kernel,
        out_shape=jax.ShapeDtypeStruct((ROWS, width), BF16),
        in_specs=[smem, smem] + [anywhere] * 4,
        out_specs=pl.BlockSpec(memory_space=pltpu.VMEM),
        scratch_shapes=[block] * 8
        + [
            pltpu.VMEM((RING, NB, BLK, HEAD), BF16),
            pltpu.VMEM((HEADS, HEAD, width), BF16),
            state, state, state,
            pltpu.VMEM((RING, HEADS, PACKED, HEAD), BF16),
            pltpu.VMEM((HEADS, RING, PACKED, HEAD), BF16),
            pltpu.VMEM((ROWS, HEADS * HEAD), BF16),
            dma((4,)), dma((6,)), dma((6,)), dma((6,)), dma((6,)), dma((10,)), dma((10,)),
            dma((RING,)), dma((HEADS,)), dma,
        ],
        compiler_params=pltpu.CompilerParams(
            collective_id=0, has_side_effects=True, vmem_limit_bytes=64 * 1024 * 1024
        ),
    )(band_width, band_offset, queries, keys, values, out_weight)


def solution(mesh):
    placed = (P("frame", "head"), P("frame", "head"), P("frame", "head"), P(), P(), P("head", None))
    return jax.shard_map(
        on_device, mesh=mesh, in_specs=placed, out_specs=P(("frame", "head"), None), check_vma=False
    )
```

```python
import functools
import math

import jax
import jax.numpy as jnp
from jax import lax
from jax.experimental import pallas as pl
from jax.experimental.pallas import tpu as pltpu
from jax.sharding import PartitionSpec as P

RING = 4
HEADS = 8
HEAD = 128
BLK = 128
NB = 4
RADIUS = 7
ROWS = 64
HALF = NB // 2
PACKED = HALF * BLK + 16
LOG2E = math.log2(math.e)
EXPONENT = LOG2E / math.sqrt(HEAD)
LOW = -1e30
MESH = pl.DeviceIdType.MESH
BF16, F32 = jnp.bfloat16, jnp.float32


def turn(value, steps):
    return lax.rem(value + (RING + steps), RING)


def kernel(
    width_ref, offset_ref, q_hbm, k_hbm, v_hbm, w_hbm, out_ref,
    k_0, k_1, k_2, k_3, v_0, v_1, v_2, v_3, q_all, w_all,
    peak_ref, total_ref, mixed_ref, packed, passing, arrived, rows_out, rows_in, sums,
    local_sem, kv_send, kv_recv, q_send, q_recv, w_send, w_recv, o_send, o_recv, a_send, a_recv,
):
    frame, head = lax.axis_index("frame"), lax.axis_index("head")
    x, z = lax.div(frame, RING), lax.rem(frame, RING)
    y, core = lax.div(head, 2), lax.rem(head, 2)

    def at(x, z, head):
        return (x * RING + z, head)

    x_next, x_last = at(turn(x, 1), z, head), at(turn(x, -1), z, head)
    z_next, z_last = at(x, turn(z, 1), head), at(x, turn(z, -1), head)
    head_next, head_last = turn(y, 1) * 2 + core, turn(y, -1) * 2 + core
    head_far, head_pair = turn(y, 2) * 2 + core, y * 2 + 1 - core
    y_next, y_last, pair = at(x, z, head_next), at(x, z, head_last), at(x, z, head_pair)
    others = [turn(y, step) * 2 + lax.rem(core + side, 2) for step in (2, 1, -1) for side in (0, 1)]
    others.append(head_pair)

    def remote(source, target, send, recv, device):
        return pltpu.make_async_remote_copy(
            src_ref=source, dst_ref=target, send_sem=send, recv_sem=recv,
            device_id=device, device_id_type=MESH,
        )

    barrier = pltpu.get_barrier_semaphore()
    greeted = [at(x, z, other) for other in others] + [x_next, x_last, z_next, z_last]
    for device in greeted:
        pl.semaphore_signal(barrier, inc=1, device_id=device, device_id_type=MESH)

    own = [
        pltpu.make_async_copy(q_hbm, q_all.at[0], local_sem.at[0]),
        pltpu.make_async_copy(k_hbm, k_0, local_sem.at[1]),
        pltpu.make_async_copy(v_hbm, v_0, local_sem.at[2]),
        pltpu.make_async_copy(w_hbm, w_all.at[head], local_sem.at[3]),
    ]
    for copy in own:
        copy.start()
    pl.semaphore_wait(barrier, len(greeted))

    kv = [
        remote(k_hbm, k_1, kv_send.at[0], kv_recv.at[0], x_next),
        remote(v_hbm, v_3, kv_send.at[1], kv_recv.at[1], x_last),
        remote(v_hbm, v_1, kv_send.at[2], kv_recv.at[2], x_next),
        remote(k_hbm, k_3, kv_send.at[3], kv_recv.at[3], x_last),
        remote(k_1, k_2, kv_send.at[4], kv_recv.at[4], x_next),
        remote(v_3, v_2, kv_send.at[5], kv_recv.at[5], x_last),
    ]
    low, high = pl.ds(0, HALF), pl.ds(HALF, HALF)
    qs = [
        remote(q_hbm.at[low], q_all.at[1, low], q_send.at[0], q_recv.at[0], z_next),
        remote(q_hbm.at[high], q_all.at[3, high], q_send.at[1], q_recv.at[1], z_last),
        remote(q_hbm.at[high], q_all.at[1, high], q_send.at[2], q_recv.at[2], z_next),
        remote(q_hbm.at[low], q_all.at[3, low], q_send.at[3], q_recv.at[3], z_last),
        remote(q_all.at[1, low], q_all.at[2, low], q_send.at[4], q_recv.at[4], z_next),
        remote(q_all.at[3, high], q_all.at[2, high], q_send.at[5], q_recv.at[5], z_last),
    ]
    top, end = pl.ds(0, HEAD // 2), pl.ds(HEAD // 2, HEAD // 2)
    ws = [
        remote(w_hbm.at[top], w_all.at[head, top], w_send.at[0], w_recv.at[0], y_next),
        remote(w_hbm.at[end], w_all.at[head, end], w_send.at[1], w_recv.at[1], y_last),
        remote(w_hbm.at[end], w_all.at[head, end], w_send.at[2], w_recv.at[2], y_next),
        remote(w_hbm.at[top], w_all.at[head, top], w_send.at[3], w_recv.at[3], y_last),
        remote(w_all.at[head_last, top], w_all.at[head_last, top], w_send.at[4], w_recv.at[4], y_next),
        remote(w_all.at[head_next, end], w_all.at[head_next, end], w_send.at[5], w_recv.at[5], y_last),
        remote(w_hbm, w_all.at[head], w_send.at[6], w_recv.at[6], pair),
        remote(w_all.at[head_last], w_all.at[head_last], w_send.at[7], w_recv.at[7], pair),
        remote(w_all.at[head_next], w_all.at[head_next], w_send.at[8], w_recv.at[8], pair),
        remote(w_all.at[head_far], w_all.at[head_far], w_send.at[9], w_recv.at[9], pair),
    ]
    os = [
        remote(packed.at[2, 0], passing.at[0], o_send.at[0], o_recv.at[0], z_next),
        remote(packed.at[2, 1], passing.at[1], o_send.at[1], o_recv.at[1], z_last),
        remote(packed.at[3], arrived.at[0], o_send.at[2], o_recv.at[2], z_next),
        remote(packed.at[1], arrived.at[1], o_send.at[3], o_recv.at[3], z_last),
        remote(passing.at[0], arrived.at[2, 0], o_send.at[4], o_recv.at[4], z_next),
        remote(passing.at[1], arrived.at[2, 1], o_send.at[5], o_recv.at[5], z_last),
    ]
    for step in range(4):
        kv[step].start()
        qs[step].start()
    for step in range(4):
        ws[step].start()
    ws[6].start()

    ones = jnp.ones((BLK, HEAD), BF16)
    tokens = NB * BLK
    key_block = lax.broadcasted_iota(jnp.int32, (1, tokens), 1) // BLK

    def query_frame(slot):
        return x * RING + turn(z, -slot)

    def wide(slot, distance, k_ref, v_ref, valid):
        this = query_frame(slot)

        def pick(block):
            past = lax.rem(key_block + (NB - offset_ref[distance, block, this]), NB)
            inside = past < width_ref[distance, this]
            inside = inside | (key_block == jnp.where(distance == 0, block, NB))
            added = jnp.where(inside, 0.0, LOW)
            if valid is not None:
                added += jnp.where(valid, 0.0, LOW)
            return k_ref[...].reshape(tokens, HEAD), v_ref[...].reshape(tokens, HEAD), added

        return NB, pick

    def narrow(slot, distance, k_ref, v_ref, valid, count):
        this = query_frame(slot)

        def pick(block):
            offset = offset_ref[distance, block, this]
            chosen = [lax.rem(offset + step, NB) for step in range(count)]
            keys, values = [k_ref[index] for index in chosen], [v_ref[index] for index in chosen]
            if count > 1:
                keys, values = [jnp.concatenate(keys, axis=0)], [jnp.concatenate(values, axis=0)]
            return keys[0], values[0], None if valid is None else jnp.where(valid, 0.0, LOW)

        return count, pick

    def join(pieces):
        return pieces[0] if len(pieces) == 1 else jnp.concatenate(pieces, axis=0)

    def attend(slot, sources, first, blocks):
        count = sum(source[0] for source in sources)
        states, scores, values = [], [], []
        for block in blocks:
            picked = [source[1](block) for source in sources]
            full = lax.dot_general(
                q_all[slot, block], join([keys for keys, _, _ in picked]), (((1,), (1,)), ((), ())),
                preferred_element_type=F32,
            )
            parts = [full[:, step * BLK:(step + 1) * BLK] for step in range(count)]
            begin = 0
            for (size, _), (_, _, added) in zip(sources, picked):
                for step in range(size):
                    if added is not None:
                        more = added[:, step * BLK:(step + 1) * BLK] if added.ndim else added
                        parts[begin + step] += more
                begin += size
            scores.append(parts)
            values.append(join([rows for _, rows, _ in picked]))
        keeps, peaks = [], []
        for block, parts in zip(blocks, scores):
            peak = jnp.max(functools.reduce(jnp.maximum, parts), axis=1, keepdims=True)
            if not first:
                before = peak_ref[slot, block]
                peak = jnp.maximum(before, peak)
                keeps.append(jnp.exp2((before - peak) * EXPONENT))
            peaks.append(peak)
        updates = []
        for parts, peak, rows in zip(scores, peaks, values):
            weights = [jnp.exp2((part - peak) * EXPONENT).astype(BF16) for part in parts]
            weights = weights[0] if count == 1 else jnp.concatenate(weights, axis=1)
            extended = jnp.concatenate([rows, join([ones] * count)], axis=1)
            updates.append(jnp.dot(weights, extended, preferred_element_type=F32))
        for index, block in enumerate(blocks):
            mixed, total = updates[index][:, :HEAD], updates[index][:, HEAD:]
            if not first:
                mixed += mixed_ref[slot, block] * keeps[index]
                total += total_ref[slot, block] * keeps[index]
            states.append((jnp.broadcast_to(peaks[index], (BLK, HEAD)), total, mixed))
        return states

    def keep(slot, states, blocks):
        for block, (peak, total, mixed) in zip(blocks, states):
            peak_ref[slot, block] = peak
            total_ref[slot, block] = total
            mixed_ref[slot, block] = mixed

    def absorb(slot, sources, first, group):
        for begin in range(0, NB, group):
            blocks = range(begin, begin + group)
            keep(slot, attend(slot, sources, first, blocks), blocks)

    row = lax.broadcasted_iota(jnp.int32, (BLK, BLK), 0)
    lane = lax.broadcasted_iota(jnp.int32, (BLK, BLK), 1)
    small_row = lax.broadcasted_iota(jnp.int32, (16, BLK), 0)

    def pack(slot, states):
        tiles = []
        for block, (peak, total, mixed) in enumerate(states):
            packed[slot, block // HALF, pl.ds(block % HALF * BLK, BLK), :] = (mixed / total).astype(BF16)
            level = peak * EXPONENT + jnp.log(total) * LOG2E
            level = jnp.sum(jnp.where(row == lane, level, 0.0), axis=0, keepdims=True)
            first = level.astype(BF16).astype(F32)
            second = (level - first).astype(BF16).astype(F32)
            tiles.append((first, second, level - first - second))
        for half in range(HALF):
            tile = jnp.zeros((16, BLK), F32)
            for index in range(HALF):
                for term in range(3):
                    tile = jnp.where(small_row == term * HALF + index, tiles[half * HALF + index][term], tile)
            packed[slot, half, pl.ds(HALF * BLK, 16), :] = tile.astype(BF16)

    every = range(NB)
    qs[0].wait_recv()
    qs[4].start()
    qs[1].wait_recv()
    qs[5].start()
    for copy in own[:3]:
        copy.wait()

    def own_keys(step, carry):
        slot = step + lax.div(step, 2) - 2 * lax.div(step, 3)

        @pl.when(step == 1)
        def _():
            kv[0].wait_recv()
            kv[4].start()
            kv[1].wait_recv()
            kv[5].start()
            qs[2].wait_recv()
            qs[3].wait_recv()

        @pl.when(step == 3)
        def _():
            ws[0].wait_recv()
            ws[4].start()
            ws[1].wait_recv()
            ws[5].start()
            qs[4].wait_recv()
            qs[5].wait_recv()

        ahead = turn(z, -slot) - z
        distance = jnp.maximum(ahead, -ahead)

        @pl.when(distance <= 1)
        def _():
            absorb(slot, [wide(slot, distance, k_0, v_0, None)], True, 2)

        @pl.when(distance >= 2)
        def _():
            absorb(slot, [narrow(slot, distance, k_0, v_0, None, 2)], True, NB)

        return carry

    lax.fori_loop(0, RING, own_keys, 0)
    kv[2].wait_recv()
    kv[3].wait_recv()

    def near_keys(slot, carry):
        ahead = turn(z, -slot) - z
        distance = jnp.maximum(ahead, -ahead)
        last, next_ = (k_1, v_1, x >= 1), (k_3, v_3, x <= RING - 2)

        @pl.when(distance == 0)
        def _():
            absorb(slot, [narrow(slot, RING, *last, 1), narrow(slot, RING, *next_, 1)], False, NB)

        for sign, near, far in ((1, next_, last), (-1, last, next_)):

            @pl.when((ahead * sign >= 1) & (ahead * sign <= 2))
            def _():
                absorb(
                    slot,
                    [
                        narrow(slot, RING - distance, *near, 2),
                        narrow(slot, RING + distance, *far, 1),
                    ],
                    False, NB,
                )

            @pl.when(ahead * sign == 3)
            def _():
                absorb(slot, [wide(slot, 1, *near), narrow(slot, RADIUS, *far, 1)], False, 2)

        return carry

    lax.fori_loop(0, RING, near_keys, 0)

    far_frame = turn(x, 2) * RING + z

    def closing(step, carry):
        late, place = lax.div(step, RING - 1), lax.rem(step, RING - 1)
        slot = lax.rem(2 + place + lax.div(place, 2), RING)
        this = query_frame(slot)
        distance = jnp.maximum(this - far_frame, far_frame - this)
        needs = distance <= RADIUS

        @pl.when(step == RING - 1)
        def _():
            kv[4].wait_recv()
            kv[5].wait_recv()

        @pl.when((late == 0) & jnp.logical_not(needs))
        def _():
            pack(slot, [(peak_ref[slot, b], total_ref[slot, b], mixed_ref[slot, b]) for b in every])

        @pl.when((late == 1) & needs)
        def _():
            pack(slot, attend(slot, [narrow(slot, distance, k_2, v_2, None, 1)], False, every))

        done = needs == (late == 1)

        @pl.when(done & (slot == 2))
        def _():
            os[0].start()
            os[1].start()

        @pl.when(done & (slot == 3))
        def _():
            os[2].start()

        @pl.when(done & (slot == 1))
        def _():
            os[3].start()

        return carry

    lax.fori_loop(0, 2 * (RING - 1), closing, 0)
    os[0].wait_recv()
    os[4].start()
    os[1].wait_recv()
    os[5].start()
    ws[2].wait_recv()
    ws[7].start()
    ws[3].wait_recv()
    ws[8].start()
    for step in range(2, 6):
        os[step].wait_recv()

    for block in every:
        half, place = block // HALF, block % HALF
        peak, total, mixed = peak_ref[0, block] * EXPONENT, total_ref[0, block], mixed_ref[0, block]
        levels = []
        for part in range(RING - 1):
            tile = arrived[part, half, pl.ds(HALF * BLK, 16), :].astype(F32)
            level = jnp.sum(jnp.where(lax.rem(small_row, HALF) == place, tile, 0.0), axis=0, keepdims=True)
            level = jnp.where(row == lane, jnp.broadcast_to(level, (BLK, BLK)), 0.0)
            levels.append(jnp.sum(level, axis=1, keepdims=True))
        top_level = jnp.maximum(functools.reduce(jnp.maximum, levels), peak)
        share = jnp.exp2(peak - top_level)
        total, mixed = total * share, mixed * share
        for part in range(RING - 1):
            share = jnp.exp2(levels[part] - top_level)
            total += share
            mixed += arrived[part, half, pl.ds(place * BLK, BLK), :].astype(F32) * share
        merged = (mixed / total).astype(BF16)
        rows_out[2 * block] = merged[:ROWS]
        rows_out[2 * block + 1] = merged[ROWS:]

    mine = pltpu.make_async_copy(rows_out.at[head], rows_in.at[head], local_sem.at[4])
    to_heads = [
        remote(rows_out.at[other], rows_in.at[head], a_send.at[index], a_recv.at[head], at(x, z, other))
        for index, other in enumerate(others)
    ]
    for copy in to_heads:
        copy.start()
    mine.start()

    ws[4].wait_recv()
    ws[5].wait_recv()
    ws[9].start()
    own[3].wait()
    mine.wait()
    for step in range(6, 9):
        ws[step].wait_recv()

    columns, tile = w_all.shape[2], 512
    for index, step in enumerate((0, -1, 1, 2)):
        chip = turn(y, step)
        if step == 2:
            ws[9].wait_recv()
        for side in range(2):
            other = chip * 2 + side

            @pl.when(other != head)
            def _():
                pltpu.make_async_copy(rows_in.at[other], rows_in.at[other], a_recv.at[other]).wait()

        left = jnp.concatenate([rows_in[chip * 2], rows_in[chip * 2 + 1]], axis=1)
        for start in range(0, columns, tile):
            weight = w_all[pl.ds(chip * 2, 2), :, start:start + tile].reshape(2 * HEAD, tile)
            term = jnp.dot(left, weight, preferred_element_type=F32)
            if index > 0:
                term += sums[:, start:start + tile]
            if index < RING - 1:
                sums[:, start:start + tile] = term
            else:
                out_ref[:, start:start + tile] = term.astype(BF16)

    for copy in kv + qs + ws + os + to_heads:
        copy.wait_send()


def on_device(queries, keys, values, band_width, band_offset, out_weight):
    width = out_weight.shape[1]
    queries, keys, values = (array.reshape(NB, BLK, HEAD) for array in (queries, keys, values))
    band_width, band_offset = band_width.T, band_offset.transpose(1, 2, 0)
    block = pltpu.VMEM((NB, BLK, HEAD), BF16)
    state = pltpu.VMEM((RING, NB, BLK, HEAD), F32)
    dma = pltpu.SemaphoreType.DMA
    smem, anywhere = pl.BlockSpec(memory_space=pltpu.SMEM), pl.BlockSpec(memory_space=pltpu.HBM)
    return pl.pallas_call(
        kernel,
        out_shape=jax.ShapeDtypeStruct((ROWS, width), BF16),
        in_specs=[smem, smem] + [anywhere] * 4,
        out_specs=pl.BlockSpec(memory_space=pltpu.VMEM),
        scratch_shapes=[block] * 8
        + [
            pltpu.VMEM((RING, NB, BLK, HEAD), BF16),
            pltpu.VMEM((HEADS, HEAD, width), BF16),
            state, state, state,
            pltpu.VMEM((RING, 2, PACKED, HEAD), BF16),
            pltpu.VMEM((2, PACKED, HEAD), BF16),
            pltpu.VMEM((RING - 1, 2, PACKED, HEAD), BF16),
            pltpu.VMEM((HEADS, ROWS, HEAD), BF16),
            pltpu.VMEM((HEADS, ROWS, HEAD), BF16),
            pltpu.VMEM((ROWS, width), F32),
            dma((5,)), dma((6,)), dma((6,)), dma((6,)), dma((6,)), dma((10,)), dma((10,)),
            dma((6,)), dma((6,)), dma((HEADS - 1,)), dma((HEADS,)),
        ],
        compiler_params=pltpu.CompilerParams(
            collective_id=0, has_side_effects=True, vmem_limit_bytes=64 * 1024 * 1024
        ),
    )(band_width, band_offset, queries, keys, values, out_weight)


def solution(mesh):
    placed = (P("frame", "head"), P("frame", "head"), P("frame", "head"), P(), P(), P("head", None))
    return jax.shard_map(
        on_device, mesh=mesh, in_specs=placed, out_specs=P(("frame", "head"), None), check_vma=False
    )
```

```python
import functools
import math

import jax
import jax.numpy as jnp
from jax import lax
from jax.experimental import pallas as pl
from jax.experimental.pallas import tpu as pltpu
from jax.sharding import PartitionSpec as P

RING = 4
HEADS = 8
HEAD = 128
BLK = 128
NB = 4
RADIUS = 7
ROWS = 64
HALF = NB // 2
PACKED = ROWS + 16
LOG2E = math.log2(math.e)
EXPONENT = LOG2E / math.sqrt(HEAD)
LOW = -1e30
MESH = pl.DeviceIdType.MESH
BF16, F32 = jnp.bfloat16, jnp.float32


def turn(value, steps):
    return lax.rem(value + (RING + steps), RING)


def kernel(
    width_ref, offset_ref, q_hbm, k_hbm, v_hbm, w_hbm, out_ref,
    k_0, k_1, k_2, k_3, v_0, v_1, v_2, v_3, q_all, w_all,
    peak_ref, total_ref, mixed_ref, packed, arrived, sums,
    local_sem, kv_send, kv_recv, q_send, q_recv, w_send, w_recv, o_send, o_recv, ready,
):
    frame, head = lax.axis_index("frame"), lax.axis_index("head")
    x, z = lax.div(frame, RING), lax.rem(frame, RING)
    y, core = lax.div(head, 2), lax.rem(head, 2)

    def at(x, z, head):
        return (x * RING + z, head)

    x_next, x_last = at(turn(x, 1), z, head), at(turn(x, -1), z, head)
    z_next, z_last = at(x, turn(z, 1), head), at(x, turn(z, -1), head)
    head_next, head_last = turn(y, 1) * 2 + core, turn(y, -1) * 2 + core
    head_far, head_pair = turn(y, 2) * 2 + core, y * 2 + 1 - core
    y_next, y_last, pair = at(x, z, head_next), at(x, z, head_last), at(x, z, head_pair)
    def remote(source, target, send, recv, device):
        return pltpu.make_async_remote_copy(
            src_ref=source, dst_ref=target, send_sem=send, recv_sem=recv,
            device_id=device, device_id_type=MESH,
        )

    barrier = pltpu.get_barrier_semaphore()
    greeted = [x_next, x_last, z_next, z_last, y_next, y_last, pair]
    for device in greeted:
        pl.semaphore_signal(barrier, inc=1, device_id=device, device_id_type=MESH)

    def announce(turn_, devices):
        for device in devices:
            pl.semaphore_signal(ready.at[turn_], inc=1, device_id=device, device_id_type=MESH)

    own = [
        pltpu.make_async_copy(q_hbm, q_all.at[0], local_sem.at[0]),
        pltpu.make_async_copy(k_hbm, k_0, local_sem.at[1]),
        pltpu.make_async_copy(v_hbm, v_0, local_sem.at[2]),
        pltpu.make_async_copy(w_hbm, w_all.at[head], local_sem.at[3]),
    ]
    for copy in own:
        copy.start()
    pl.semaphore_wait(barrier, len(greeted))

    kv = [
        remote(k_hbm, k_1, kv_send.at[0], kv_recv.at[0], x_next),
        remote(v_hbm, v_3, kv_send.at[1], kv_recv.at[1], x_last),
        remote(v_hbm, v_1, kv_send.at[2], kv_recv.at[2], x_next),
        remote(k_hbm, k_3, kv_send.at[3], kv_recv.at[3], x_last),
        remote(k_1, k_2, kv_send.at[4], kv_recv.at[4], x_next),
        remote(v_3, v_2, kv_send.at[5], kv_recv.at[5], x_last),
    ]
    low, high = pl.ds(0, HALF), pl.ds(HALF, HALF)
    qs = [
        remote(q_hbm.at[low], q_all.at[1, low], q_send.at[0], q_recv.at[0], z_next),
        remote(q_hbm.at[high], q_all.at[3, high], q_send.at[1], q_recv.at[1], z_last),
        remote(q_hbm.at[high], q_all.at[1, high], q_send.at[2], q_recv.at[2], z_next),
        remote(q_hbm.at[low], q_all.at[3, low], q_send.at[3], q_recv.at[3], z_last),
        remote(q_all.at[1, low], q_all.at[2, low], q_send.at[4], q_recv.at[4], z_next),
        remote(q_all.at[3, high], q_all.at[2, high], q_send.at[5], q_recv.at[5], z_last),
    ]
    top, end = pl.ds(0, HEAD // 2), pl.ds(HEAD // 2, HEAD // 2)
    ws = [
        remote(w_hbm.at[top], w_all.at[head, top], w_send.at[0], w_recv.at[0], y_next),
        remote(w_hbm.at[end], w_all.at[head, end], w_send.at[1], w_recv.at[1], y_last),
        remote(w_hbm.at[end], w_all.at[head, end], w_send.at[2], w_recv.at[2], y_next),
        remote(w_hbm.at[top], w_all.at[head, top], w_send.at[3], w_recv.at[3], y_last),
        remote(w_all.at[head_last, top], w_all.at[head_last, top], w_send.at[4], w_recv.at[4], y_next),
        remote(w_all.at[head_next, end], w_all.at[head_next, end], w_send.at[5], w_recv.at[5], y_last),
        remote(w_hbm, w_all.at[head], w_send.at[6], w_recv.at[6], pair),
        remote(w_all.at[head_last], w_all.at[head_last], w_send.at[7], w_recv.at[7], pair),
        remote(w_all.at[head_next], w_all.at[head_next], w_send.at[8], w_recv.at[8], pair),
        remote(w_all.at[head_far], w_all.at[head_far], w_send.at[9], w_recv.at[9], pair),
    ]
    for step in range(4):
        kv[step].start()
        qs[step].start()
    for step in range(4):
        ws[step].start()
    ws[6].start()
    announce(0, (z_next, z_last))

    ones = jnp.ones((BLK, HEAD), BF16)
    tokens = NB * BLK
    key_block = lax.broadcasted_iota(jnp.int32, (1, tokens), 1) // BLK

    def query_frame(slot):
        return x * RING + turn(z, -slot)

    def wide(slot, distance, k_ref, v_ref, valid):
        this = query_frame(slot)

        def pick(block):
            past = lax.rem(key_block + (NB - offset_ref[distance, block, this]), NB)
            inside = past < width_ref[distance, this]
            inside = inside | (key_block == jnp.where(distance == 0, block, NB))
            added = jnp.where(inside, 0.0, LOW)
            if valid is not None:
                added += jnp.where(valid, 0.0, LOW)
            return k_ref[...].reshape(tokens, HEAD), v_ref[...].reshape(tokens, HEAD), added

        return NB, pick

    def narrow(slot, distance, k_ref, v_ref, valid, count):
        this = query_frame(slot)

        def pick(block):
            offset = offset_ref[distance, block, this]
            chosen = [lax.rem(offset + step, NB) for step in range(count)]
            keys, values = [k_ref[index] for index in chosen], [v_ref[index] for index in chosen]
            if count > 1:
                keys, values = [jnp.concatenate(keys, axis=0)], [jnp.concatenate(values, axis=0)]
            return keys[0], values[0], None if valid is None else jnp.where(valid, 0.0, LOW)

        return count, pick

    def join(pieces):
        return pieces[0] if len(pieces) == 1 else jnp.concatenate(pieces, axis=0)

    def attend(slot, sources, first, blocks):
        count = sum(source[0] for source in sources)
        states, scores, values = [], [], []
        for block in blocks:
            picked = [source[1](block) for source in sources]
            full = lax.dot_general(
                q_all[slot, block], join([keys for keys, _, _ in picked]), (((1,), (1,)), ((), ())),
                preferred_element_type=F32,
            )
            parts = [full[:, step * BLK:(step + 1) * BLK] for step in range(count)]
            begin = 0
            for (size, _), (_, _, added) in zip(sources, picked):
                for step in range(size):
                    if added is not None:
                        more = added[:, step * BLK:(step + 1) * BLK] if added.ndim else added
                        parts[begin + step] += more
                begin += size
            scores.append(parts)
            values.append(join([rows for _, rows, _ in picked]))
        keeps, peaks = [], []
        for block, parts in zip(blocks, scores):
            peak = jnp.max(functools.reduce(jnp.maximum, parts), axis=1, keepdims=True)
            if not first:
                before = peak_ref[slot, block]
                peak = jnp.maximum(before, peak)
                keeps.append(jnp.exp2((before - peak) * EXPONENT))
            peaks.append(peak)
        updates = []
        for parts, peak, rows in zip(scores, peaks, values):
            weights = [jnp.exp2((part - peak) * EXPONENT).astype(BF16) for part in parts]
            weights = weights[0] if count == 1 else jnp.concatenate(weights, axis=1)
            extended = jnp.concatenate([rows, join([ones] * count)], axis=1)
            updates.append(jnp.dot(weights, extended, preferred_element_type=F32))
        for index, block in enumerate(blocks):
            mixed, total = updates[index][:, :HEAD], updates[index][:, HEAD:]
            if not first:
                mixed += mixed_ref[slot, block] * keeps[index]
                total += total_ref[slot, block] * keeps[index]
            states.append((jnp.broadcast_to(peaks[index], (BLK, HEAD)), total, mixed))
        return states

    def keep(slot, states, blocks):
        for block, (peak, total, mixed) in zip(blocks, states):
            peak_ref[slot, block] = peak
            total_ref[slot, block] = total
            mixed_ref[slot, block] = mixed

    def absorb(slot, sources, first, group):
        for begin in range(0, NB, group):
            blocks = range(begin, begin + group)
            keep(slot, attend(slot, sources, first, blocks), blocks)

    row = lax.broadcasted_iota(jnp.int32, (BLK, BLK), 0)
    lane = lax.broadcasted_iota(jnp.int32, (BLK, BLK), 1)
    small_row = lax.broadcasted_iota(jnp.int32, (16, BLK), 0)

    def pack(slot, states):
        for block, (peak, total, mixed) in enumerate(states):
            scaled = (mixed / total).astype(BF16)
            level = peak * EXPONENT + jnp.log(total) * LOG2E
            level = jnp.sum(jnp.where(row == lane, level, 0.0), axis=0, keepdims=True)
            first = level.astype(BF16).astype(F32)
            second = (level - first).astype(BF16).astype(F32)
            tile = jnp.where(
                small_row == 0, first,
                jnp.where(small_row == 1, second, jnp.where(small_row == 2, level - first - second, 0.0)),
            ).astype(BF16)
            for half in range(2):
                packed[slot, 2 * block + half, 0:ROWS, :] = scaled[half * ROWS:(half + 1) * ROWS]
                packed[slot, 2 * block + half, ROWS:PACKED, :] = tile

    def send(slot):
        def each(step, carry):
            receiver = lax.rem(2 * y + RING + step, HEADS)
            source, target = packed.at[slot, receiver], arrived.at[head, z]
            here = (slot == 0) & (receiver == head)

            @pl.when(here)
            def _():
                pltpu.make_async_copy(source, target, local_sem.at[4]).start()

            @pl.when(jnp.logical_not(here))
            def _():
                remote(
                    source, target, o_send.at[slot], o_recv.at[head], at(x, turn(z, -slot), receiver)
                ).start()

            return carry

        lax.fori_loop(0, HEADS, each, 0)

    every = range(NB)
    qs[0].wait_recv()
    qs[4].start()
    qs[1].wait_recv()
    qs[5].start()
    for copy in own[:3]:
        copy.wait()
    pl.semaphore_wait(ready.at[0], 2)
    announce(1, (y_next, y_last))

    def own_keys(step, carry):
        slot = step + lax.div(step, 2) - 2 * lax.div(step, 3)

        @pl.when(step == 1)
        def _():
            kv[0].wait_recv()
            kv[4].start()
            kv[1].wait_recv()
            kv[5].start()
            qs[2].wait_recv()
            qs[3].wait_recv()
            pl.semaphore_wait(ready.at[1], 2)
            announce(2, (y_next, y_last))

        @pl.when(step == 3)
        def _():
            ws[0].wait_recv()
            ws[4].start()
            ws[1].wait_recv()
            ws[5].start()
            qs[4].wait_recv()
            qs[5].wait_recv()
            pl.semaphore_wait(ready.at[2], 2)
            announce(3, (pair,))

        ahead = turn(z, -slot) - z
        distance = jnp.maximum(ahead, -ahead)

        @pl.when(distance <= 1)
        def _():
            absorb(slot, [wide(slot, distance, k_0, v_0, None)], True, 2)

        @pl.when(distance >= 2)
        def _():
            absorb(slot, [narrow(slot, distance, k_0, v_0, None, 2)], True, NB)

        return carry

    lax.fori_loop(0, RING, own_keys, 0)
    kv[2].wait_recv()
    kv[3].wait_recv()

    def near_keys(slot, carry):
        ahead = turn(z, -slot) - z
        distance = jnp.maximum(ahead, -ahead)
        last, next_ = (k_1, v_1, x >= 1), (k_3, v_3, x <= RING - 2)

        @pl.when(distance == 0)
        def _():
            absorb(slot, [narrow(slot, RING, *last, 1), narrow(slot, RING, *next_, 1)], False, NB)

        for sign, near, far in ((1, next_, last), (-1, last, next_)):

            @pl.when((ahead * sign >= 1) & (ahead * sign <= 2))
            def _():
                absorb(
                    slot,
                    [
                        narrow(slot, RING - distance, *near, 2),
                        narrow(slot, RING + distance, *far, 1),
                    ],
                    False, NB,
                )

            @pl.when(ahead * sign == 3)
            def _():
                absorb(slot, [wide(slot, 1, *near), narrow(slot, RADIUS, *far, 1)], False, 2)

        return carry

    lax.fori_loop(0, RING, near_keys, 0)

    pl.semaphore_wait(ready.at[3], 1)
    far_frame = turn(x, 2) * RING + z

    def closing(step, carry):
        late, place = lax.div(step, RING), lax.rem(step, RING)
        slot = lax.rem(2 + 3 * place + 3 * lax.div(place, 2) + 2 * lax.div(place, 3), RING)
        this = query_frame(slot)
        distance = jnp.maximum(this - far_frame, far_frame - this)
        needs = distance <= RADIUS

        @pl.when(step == RING)
        def _():
            kv[4].wait_recv()
            kv[5].wait_recv()

        @pl.when((late == 0) & jnp.logical_not(needs))
        def _():
            pack(slot, [(peak_ref[slot, b], total_ref[slot, b], mixed_ref[slot, b]) for b in every])

        @pl.when((late == 1) & needs)
        def _():
            pack(slot, attend(slot, [narrow(slot, distance, k_2, v_2, None, 1)], False, every))

        @pl.when(needs == (late == 1))
        def _():
            send(slot)

        return carry

    lax.fori_loop(0, 2 * RING, closing, 0)
    ws[2].wait_recv()
    ws[7].start()
    ws[3].wait_recv()
    ws[8].start()
    ws[4].wait_recv()
    ws[5].wait_recv()
    ws[9].start()

    column = lax.broadcasted_iota(jnp.int32, (ROWS, HEAD), 1)
    here = lax.broadcasted_iota(jnp.int32, (ROWS, HEAD), 0) + core * ROWS

    def merge(other):
        levels = []
        for part in range(RING):
            tile = arrived[other, part, ROWS:PACKED, :].astype(F32)
            levels.append(jnp.sum(tile, axis=0, keepdims=True))
        peak = functools.reduce(jnp.maximum, levels)
        shares = [jnp.exp2(level - peak) for level in levels]
        whole = functools.reduce(jnp.add, shares)
        merged = jnp.zeros((ROWS, HEAD), F32)
        for part in range(RING):
            share = jnp.broadcast_to(shares[part] / whole, (ROWS, HEAD))
            share = jnp.sum(jnp.where(column == here, share, 0.0), axis=1, keepdims=True)
            merged += arrived[other, part, 0:ROWS, :].astype(F32) * share
        return merged.astype(BF16)

    pltpu.make_async_copy(packed.at[0, head], arrived.at[head, z], local_sem.at[4]).wait()
    own[3].wait()
    for step in range(6, 9):
        ws[step].wait_recv()

    columns, tile = w_all.shape[2], 512
    for index, step in enumerate((0, -1, 1, 2)):
        chip = turn(y, step)
        if step == 2:
            ws[9].wait_recv()
        for side in range(2):
            other = chip * 2 + side

            @pl.when(other == head)
            def _():
                three = arrived.at[other, pl.ds(0, RING - 1)]
                pltpu.make_async_copy(three, three, o_recv.at[other]).wait()

            @pl.when(other != head)
            def _():
                pltpu.make_async_copy(arrived.at[other], arrived.at[other], o_recv.at[other]).wait()

        left = jnp.concatenate([merge(chip * 2), merge(chip * 2 + 1)], axis=1)
        for start in range(0, columns, tile):
            weight = w_all[pl.ds(chip * 2, 2), :, start:start + tile].reshape(2 * HEAD, tile)
            term = jnp.dot(left, weight, preferred_element_type=F32)
            if index > 0:
                term += sums[:, start:start + tile]
            if index < RING - 1:
                sums[:, start:start + tile] = term
            else:
                out_ref[:, start:start + tile] = term

    for copy in kv + qs + ws:
        copy.wait_send()
    seven = packed.at[0, pl.ds(0, HEADS - 1)]
    pltpu.make_async_copy(seven, seven, o_send.at[0]).wait()
    for slot in range(1, RING):
        pltpu.make_async_copy(packed.at[slot], packed.at[slot], o_send.at[slot]).wait()


def on_device(queries, keys, values, band_width, band_offset, out_weight):
    width = out_weight.shape[1]
    queries, keys, values = (array.reshape(NB, BLK, HEAD) for array in (queries, keys, values))
    band_width, band_offset = band_width.T, band_offset.transpose(1, 2, 0)
    block = pltpu.VMEM((NB, BLK, HEAD), BF16)
    state = pltpu.VMEM((RING, NB, BLK, HEAD), F32)
    dma = pltpu.SemaphoreType.DMA
    smem, anywhere = pl.BlockSpec(memory_space=pltpu.SMEM), pl.BlockSpec(memory_space=pltpu.HBM)
    return pl.pallas_call(
        kernel,
        out_shape=jax.ShapeDtypeStruct((ROWS, width), F32),
        in_specs=[smem, smem] + [anywhere] * 4,
        out_specs=pl.BlockSpec(memory_space=pltpu.VMEM),
        scratch_shapes=[block] * 8
        + [
            pltpu.VMEM((RING, NB, BLK, HEAD), BF16),
            pltpu.VMEM((HEADS, HEAD, width), BF16),
            state, state, state,
            pltpu.VMEM((RING, HEADS, PACKED, HEAD), BF16),
            pltpu.VMEM((HEADS, RING, PACKED, HEAD), BF16),
            pltpu.VMEM((ROWS, width), F32),
            dma((5,)), dma((6,)), dma((6,)), dma((6,)), dma((6,)), dma((10,)), dma((10,)),
            dma((RING,)), dma((HEADS,)), pltpu.SemaphoreType.REGULAR((4,)),
        ],
        compiler_params=pltpu.CompilerParams(
            collective_id=0, has_side_effects=True, vmem_limit_bytes=64 * 1024 * 1024
        ),
    )(band_width, band_offset, queries, keys, values, out_weight).astype(BF16)


def solution(mesh):
    placed = (P("frame", "head"), P("frame", "head"), P("frame", "head"), P(), P(), P("head", None))
    return jax.shard_map(
        on_device, mesh=mesh, in_specs=placed, out_specs=P(("frame", "head"), None), check_vma=False
    )
```

```python
import functools
import math

import jax
import jax.numpy as jnp
from jax import lax
from jax.experimental import pallas as pl
from jax.experimental.pallas import tpu as pltpu
from jax.sharding import PartitionSpec as P

RING = 4
HEADS = 8
HEAD = 128
BLK = 128
NB = 4
RADIUS = 7
ROWS = 64
HALF = NB // 2
PACKED = ROWS + 16
LOG2E = math.log2(math.e)
EXPONENT = LOG2E / math.sqrt(HEAD)
LOW = -1e30
MESH = pl.DeviceIdType.MESH
BF16, F32 = jnp.bfloat16, jnp.float32


def turn(value, steps):
    return lax.rem(value + (RING + steps), RING)


def kernel(
    width_ref, offset_ref, q_hbm, k_hbm, v_hbm, w_hbm, out_ref,
    k_0, k_1, k_2, k_3, v_0, v_1, v_2, v_3, q_all, w_all,
    peak_ref, total_ref, mixed_ref, packed, arrived, sums,
    local_sem, kv_send, kv_recv, q_send, q_recv, w_send, w_recv, o_send, o_recv, ready,
):
    frame, head = lax.axis_index("frame"), lax.axis_index("head")
    x, z = lax.div(frame, RING), lax.rem(frame, RING)
    y, core = lax.div(head, 2), lax.rem(head, 2)

    def at(x, z, head):
        return (x * RING + z, head)

    x_next, x_last = at(turn(x, 1), z, head), at(turn(x, -1), z, head)
    z_next, z_last = at(x, turn(z, 1), head), at(x, turn(z, -1), head)
    head_next, head_last = turn(y, 1) * 2 + core, turn(y, -1) * 2 + core
    head_far, head_pair = turn(y, 2) * 2 + core, y * 2 + 1 - core
    y_next, y_last, pair = at(x, z, head_next), at(x, z, head_last), at(x, z, head_pair)
    def remote(source, target, send, recv, device):
        return pltpu.make_async_remote_copy(
            src_ref=source, dst_ref=target, send_sem=send, recv_sem=recv,
            device_id=device, device_id_type=MESH,
        )

    barrier = pltpu.get_barrier_semaphore()
    greeted = [x_next, x_last, z_next, z_last, y_next, y_last, pair]
    for device in greeted:
        pl.semaphore_signal(barrier, inc=1, device_id=device, device_id_type=MESH)

    def announce(turn_, devices):
        for device in devices:
            pl.semaphore_signal(ready.at[turn_], inc=1, device_id=device, device_id_type=MESH)

    own = [
        pltpu.make_async_copy(q_hbm, q_all.at[0], local_sem.at[0]),
        pltpu.make_async_copy(k_hbm, k_0, local_sem.at[1]),
        pltpu.make_async_copy(v_hbm, v_0, local_sem.at[2]),
        pltpu.make_async_copy(w_hbm, w_all.at[head], local_sem.at[3]),
    ]
    for copy in own:
        copy.start()
    pl.semaphore_wait(barrier, len(greeted))

    kv = [
        remote(k_hbm, k_1, kv_send.at[0], kv_recv.at[0], x_next),
        remote(v_hbm, v_3, kv_send.at[1], kv_recv.at[1], x_last),
        remote(v_hbm, v_1, kv_send.at[2], kv_recv.at[2], x_next),
        remote(k_hbm, k_3, kv_send.at[3], kv_recv.at[3], x_last),
        remote(k_1, k_2, kv_send.at[4], kv_recv.at[4], x_next),
        remote(v_3, v_2, kv_send.at[5], kv_recv.at[5], x_last),
    ]
    low, high = pl.ds(0, HALF), pl.ds(HALF, HALF)
    qs = [
        remote(q_hbm.at[low], q_all.at[1, low], q_send.at[0], q_recv.at[0], z_next),
        remote(q_hbm.at[high], q_all.at[3, high], q_send.at[1], q_recv.at[1], z_last),
        remote(q_hbm.at[high], q_all.at[1, high], q_send.at[2], q_recv.at[2], z_next),
        remote(q_hbm.at[low], q_all.at[3, low], q_send.at[3], q_recv.at[3], z_last),
        remote(q_all.at[1, low], q_all.at[2, low], q_send.at[4], q_recv.at[4], z_next),
        remote(q_all.at[3, high], q_all.at[2, high], q_send.at[5], q_recv.at[5], z_last),
    ]
    part_rows = HEAD // RING

    def quarter(which, begin=0, size=part_rows):
        return pl.ds(pl.multiple_of(which * part_rows + begin, part_rows // 2), size)

    def weights(source, shard, rows, sem, device, send=None):
        return remote(
            source, w_all.at[shard, rows], w_send.at[sem if send is None else send], w_recv.at[sem], device
        )

    half_rows, later = part_rows // 2, HEAD - part_rows
    direct = [
        weights(w_hbm.at[quarter(turn(x, step))], head, quarter(turn(x, step)), side + min(step, 1), device)
        for step in range(RING) for side, device in ((0, y_next), (2, y_last))
    ]

    def passed(shard, which, begin, size, sem, device):
        rows = quarter(which, begin, size)
        return weights(w_all.at[shard, rows], shard, rows, sem, device)

    every_row = pl.ds(0, HEAD)
    ws = {
        4: passed(head_last, x, 0, half_rows, 4, y_next),
        5: passed(head_next, x, half_rows, half_rows, 5, y_last),
        6: passed(head_far, x, 0, part_rows, 6, x_next),
        7: passed(head_far, x, 0, part_rows, 7, x_last),
        8: passed(head_far, turn(x, -1), 0, half_rows, 8, x_next),
        9: passed(head_far, turn(x, 1), half_rows, half_rows, 9, x_last),
        10: weights(w_hbm, head, every_row, 10, pair),
        11: weights(w_all.at[head_last], head_last, every_row, 11, pair),
        12: weights(w_all.at[head_next], head_next, every_row, 12, pair),
        13: weights(w_all.at[head_far], head_far, every_row, 13, pair),
    }
    several = w_all.at[head, pl.ds(0, later)]
    for step in range(4):
        kv[step].start()
        qs[step].start()
    for copy in direct[:6]:
        copy.start()
    ws[10].start()
    announce(0, (z_next, z_last))

    ones = jnp.ones((BLK, HEAD), BF16)
    tokens = NB * BLK
    key_block = lax.broadcasted_iota(jnp.int32, (1, tokens), 1) // BLK

    def query_frame(slot):
        return x * RING + turn(z, -slot)

    def wide(slot, distance, k_ref, v_ref, valid):
        this = query_frame(slot)

        def pick(block):
            past = lax.rem(key_block + (NB - offset_ref[distance, block, this]), NB)
            inside = past < width_ref[distance, this]
            inside = inside | (key_block == jnp.where(distance == 0, block, NB))
            added = jnp.where(inside, 0.0, LOW)
            if valid is not None:
                added += jnp.where(valid, 0.0, LOW)
            return k_ref[...].reshape(tokens, HEAD), v_ref[...].reshape(tokens, HEAD), added

        return NB, pick

    def narrow(slot, distance, k_ref, v_ref, valid, count):
        this = query_frame(slot)

        def pick(block):
            offset = offset_ref[distance, block, this]
            chosen = [lax.rem(offset + step, NB) for step in range(count)]
            keys, values = [k_ref[index] for index in chosen], [v_ref[index] for index in chosen]
            if count > 1:
                keys, values = [jnp.concatenate(keys, axis=0)], [jnp.concatenate(values, axis=0)]
            return keys[0], values[0], None if valid is None else jnp.where(valid, 0.0, LOW)

        return count, pick

    def join(pieces):
        return pieces[0] if len(pieces) == 1 else jnp.concatenate(pieces, axis=0)

    def attend(slot, sources, first, blocks):
        count = sum(source[0] for source in sources)
        states, scores, values = [], [], []
        for block in blocks:
            picked = [source[1](block) for source in sources]
            full = lax.dot_general(
                q_all[slot, block], join([keys for keys, _, _ in picked]), (((1,), (1,)), ((), ())),
                preferred_element_type=F32,
            )
            parts = [full[:, step * BLK:(step + 1) * BLK] for step in range(count)]
            begin = 0
            for (size, _), (_, _, added) in zip(sources, picked):
                for step in range(size):
                    if added is not None:
                        more = added[:, step * BLK:(step + 1) * BLK] if added.ndim else added
                        parts[begin + step] += more
                begin += size
            scores.append(parts)
            values.append(join([rows for _, rows, _ in picked]))
        keeps, peaks = [], []
        for block, parts in zip(blocks, scores):
            peak = jnp.max(functools.reduce(jnp.maximum, parts), axis=1, keepdims=True)
            if not first:
                before = peak_ref[slot, block]
                peak = jnp.maximum(before, peak)
                keeps.append(jnp.exp2((before - peak) * EXPONENT))
            peaks.append(peak)
        updates = []
        for parts, peak, rows in zip(scores, peaks, values):
            weights = [jnp.exp2((part - peak) * EXPONENT).astype(BF16) for part in parts]
            weights = weights[0] if count == 1 else jnp.concatenate(weights, axis=1)
            extended = jnp.concatenate([rows, join([ones] * count)], axis=1)
            updates.append(jnp.dot(weights, extended, preferred_element_type=F32))
        for index, block in enumerate(blocks):
            mixed, total = updates[index][:, :HEAD], updates[index][:, HEAD:]
            if not first:
                mixed += mixed_ref[slot, block] * keeps[index]
                total += total_ref[slot, block] * keeps[index]
            states.append((jnp.broadcast_to(peaks[index], (BLK, HEAD)), total, mixed))
        return states

    def keep(slot, states, blocks):
        for block, (peak, total, mixed) in zip(blocks, states):
            peak_ref[slot, block] = peak
            total_ref[slot, block] = total
            mixed_ref[slot, block] = mixed

    def absorb(slot, sources, first, group):
        for begin in range(0, NB, group):
            blocks = range(begin, begin + group)
            keep(slot, attend(slot, sources, first, blocks), blocks)

    row = lax.broadcasted_iota(jnp.int32, (BLK, BLK), 0)
    lane = lax.broadcasted_iota(jnp.int32, (BLK, BLK), 1)
    small_row = lax.broadcasted_iota(jnp.int32, (16, BLK), 0)

    def pack(slot, states):
        for block, (peak, total, mixed) in enumerate(states):
            scaled = (mixed / total).astype(BF16)
            level = peak * EXPONENT + jnp.log(total) * LOG2E
            level = jnp.sum(jnp.where(row == lane, level, 0.0), axis=0, keepdims=True)
            first = level.astype(BF16).astype(F32)
            second = (level - first).astype(BF16).astype(F32)
            tile = jnp.where(
                small_row == 0, first,
                jnp.where(small_row == 1, second, jnp.where(small_row == 2, level - first - second, 0.0)),
            ).astype(BF16)
            for half in range(2):
                packed[slot, 2 * block + half, 0:ROWS, :] = scaled[half * ROWS:(half + 1) * ROWS]
                packed[slot, 2 * block + half, ROWS:PACKED, :] = tile

    def send(slot):
        def each(step, carry):
            receiver = lax.rem(2 * y + RING + step, HEADS)
            source, target = packed.at[slot, receiver], arrived.at[head, z]
            here = (slot == 0) & (receiver == head)

            @pl.when(here)
            def _():
                pltpu.make_async_copy(source, target, local_sem.at[4]).start()

            @pl.when(jnp.logical_not(here))
            def _():
                remote(
                    source, target, o_send.at[slot], o_recv.at[head], at(x, turn(z, -slot), receiver)
                ).start()

            return carry

        lax.fori_loop(0, HEADS, each, 0)

    every = range(NB)
    qs[0].wait_recv()
    qs[4].start()
    qs[1].wait_recv()
    qs[5].start()
    for copy in own[:3]:
        copy.wait()
    pl.semaphore_wait(ready.at[0], 2)
    announce(1, (y_next, y_last))

    def own_keys(step, carry):
        slot = step + lax.div(step, 2) - 2 * lax.div(step, 3)

        @pl.when(step == 1)
        def _():
            kv[0].wait_recv()
            kv[4].start()
            kv[1].wait_recv()
            kv[5].start()
            qs[2].wait_recv()
            qs[3].wait_recv()
            direct[0].wait_recv()
            ws[4].start()
            direct[1].wait_recv()
            ws[5].start()
            for copy in direct[6:]:
                copy.start()
            pl.semaphore_wait(ready.at[1], 2)
            announce(2, (y_next, y_last))

        @pl.when(step == 3)
        def _():
            qs[4].wait_recv()
            qs[5].wait_recv()
            pl.semaphore_wait(ready.at[2], 2)
            announce(3, (pair,))

        ahead = turn(z, -slot) - z
        distance = jnp.maximum(ahead, -ahead)

        @pl.when(distance <= 1)
        def _():
            absorb(slot, [wide(slot, distance, k_0, v_0, None)], True, 2)

        @pl.when(distance >= 2)
        def _():
            absorb(slot, [narrow(slot, distance, k_0, v_0, None, 2)], True, NB)

        return carry

    lax.fori_loop(0, RING, own_keys, 0)
    kv[2].wait_recv()
    kv[3].wait_recv()

    def near_keys(slot, carry):
        ahead = turn(z, -slot) - z
        distance = jnp.maximum(ahead, -ahead)
        last, next_ = (k_1, v_1, x >= 1), (k_3, v_3, x <= RING - 2)

        @pl.when(distance == 0)
        def _():
            absorb(slot, [narrow(slot, RING, *last, 1), narrow(slot, RING, *next_, 1)], False, NB)

        for sign, near, far in ((1, next_, last), (-1, last, next_)):

            @pl.when((ahead * sign >= 1) & (ahead * sign <= 2))
            def _():
                absorb(
                    slot,
                    [
                        narrow(slot, RING - distance, *near, 2),
                        narrow(slot, RING + distance, *far, 1),
                    ],
                    False, NB,
                )

            @pl.when(ahead * sign == 3)
            def _():
                absorb(slot, [wide(slot, 1, *near), narrow(slot, RADIUS, *far, 1)], False, 2)

        return carry

    lax.fori_loop(0, RING, near_keys, 0)

    ws[4].wait_recv()
    ws[5].wait_recv()
    ws[6].start()
    ws[7].start()
    pl.semaphore_wait(ready.at[3], 1)
    far_frame = turn(x, 2) * RING + z

    def far_keys(slot):
        this = query_frame(slot)
        distance = jnp.maximum(this - far_frame, far_frame - this)
        source = narrow(slot, jnp.minimum(distance, RADIUS), k_2, v_2, distance <= RADIUS, 1)
        return attend(slot, [source], False, every)

    pack(0, [(peak_ref[0, b], total_ref[0, b], mixed_ref[0, b]) for b in every])
    send(0)
    kv[4].wait_recv()
    kv[5].wait_recv()
    pack(2, far_keys(2))
    send(2)
    states = far_keys(3), far_keys(1)
    pack(3, states[0])
    pack(1, states[1])
    send(3)
    send(1)
    ws[6].wait_recv()
    ws[8].start()
    ws[7].wait_recv()
    ws[9].start()
    pltpu.make_async_copy(several, several, w_recv.at[1]).wait()
    ws[11].start()
    pltpu.make_async_copy(several, several, w_recv.at[3]).wait()
    ws[12].start()
    ws[8].wait_recv()
    ws[9].wait_recv()
    ws[13].start()

    column = lax.broadcasted_iota(jnp.int32, (ROWS, HEAD), 1)
    here = lax.broadcasted_iota(jnp.int32, (ROWS, HEAD), 0) + core * ROWS

    def merge(other):
        levels = []
        for part in range(RING):
            tile = arrived[other, part, ROWS:PACKED, :].astype(F32)
            levels.append(jnp.sum(tile, axis=0, keepdims=True))
        peak = functools.reduce(jnp.maximum, levels)
        shares = [jnp.exp2(level - peak) for level in levels]
        whole = functools.reduce(jnp.add, shares)
        merged = jnp.zeros((ROWS, HEAD), F32)
        for part in range(RING):
            share = jnp.broadcast_to(shares[part] / whole, (ROWS, HEAD))
            share = jnp.sum(jnp.where(column == here, share, 0.0), axis=1, keepdims=True)
            merged += arrived[other, part, 0:ROWS, :].astype(F32) * share
        return merged.astype(BF16)

    pltpu.make_async_copy(packed.at[0, head], arrived.at[head, z], local_sem.at[4]).wait()
    own[3].wait()
    for step in range(10, 13):
        ws[step].wait_recv()

    columns, tile = w_all.shape[2], 512
    for index, step in enumerate((0, -1, 1, 2)):
        chip = turn(y, step)
        if step == 2:
            ws[13].wait_recv()
        for side in range(2):
            other = chip * 2 + side

            @pl.when(other == head)
            def _():
                three = arrived.at[other, pl.ds(0, RING - 1)]
                pltpu.make_async_copy(three, three, o_recv.at[other]).wait()

            @pl.when(other != head)
            def _():
                pltpu.make_async_copy(arrived.at[other], arrived.at[other], o_recv.at[other]).wait()

        left = jnp.concatenate([merge(chip * 2), merge(chip * 2 + 1)], axis=1)
        for start in range(0, columns, tile):
            weight = w_all[pl.ds(chip * 2, 2), :, start:start + tile].reshape(2 * HEAD, tile)
            term = jnp.dot(left, weight, preferred_element_type=F32)
            if index > 0:
                term += sums[:, start:start + tile]
            if index < RING - 1:
                sums[:, start:start + tile] = term
            else:
                out_ref[:, start:start + tile] = term

    for copy in kv + qs + direct[:2] + list(ws.values()):
        copy.wait_send()
    for sem in (1, 3):
        pltpu.make_async_copy(several, several, w_send.at[sem]).wait()
    seven = packed.at[0, pl.ds(0, HEADS - 1)]
    pltpu.make_async_copy(seven, seven, o_send.at[0]).wait()
    for slot in range(1, RING):
        pltpu.make_async_copy(packed.at[slot], packed.at[slot], o_send.at[slot]).wait()


def on_device(queries, keys, values, band_width, band_offset, out_weight):
    width = out_weight.shape[1]
    queries, keys, values = (array.reshape(NB, BLK, HEAD) for array in (queries, keys, values))
    band_width, band_offset = band_width.T, band_offset.transpose(1, 2, 0)
    band_width, band_offset, queries, keys, values, out_weight = (
        pltpu.with_memory_space_constraint(array, pltpu.HBM)
        for array in (band_width, band_offset, queries, keys, values, out_weight)
    )
    block = pltpu.VMEM((NB, BLK, HEAD), BF16)
    state = pltpu.VMEM((RING, NB, BLK, HEAD), F32)
    dma = pltpu.SemaphoreType.DMA
    smem, anywhere = pl.BlockSpec(memory_space=pltpu.SMEM), pl.BlockSpec(memory_space=pltpu.HBM)
    return pl.pallas_call(
        kernel,
        out_shape=jax.ShapeDtypeStruct((ROWS, width), F32),
        in_specs=[smem, smem] + [anywhere] * 4,
        out_specs=pl.BlockSpec(memory_space=pltpu.VMEM),
        scratch_shapes=[block] * 8
        + [
            pltpu.VMEM((RING, NB, BLK, HEAD), BF16),
            pltpu.VMEM((HEADS, HEAD, width), BF16),
            state, state, state,
            pltpu.VMEM((RING, HEADS, PACKED, HEAD), BF16),
            pltpu.VMEM((HEADS, RING, PACKED, HEAD), BF16),
            pltpu.VMEM((ROWS, width), F32),
            dma((5,)), dma((6,)), dma((6,)), dma((6,)), dma((6,)), dma((14,)), dma((14,)),
            dma((RING,)), dma((HEADS,)), pltpu.SemaphoreType.REGULAR((4,)),
        ],
        compiler_params=pltpu.CompilerParams(
            collective_id=0, has_side_effects=True, vmem_limit_bytes=52 * 1024 * 1024
        ),
    )(band_width, band_offset, queries, keys, values, out_weight).astype(BF16)


def solution(mesh):
    placed = (P("frame", "head"), P("frame", "head"), P("frame", "head"), P(), P(), P("head", None))
    return jax.shard_map(
        on_device, mesh=mesh, in_specs=placed, out_specs=P(("frame", "head"), None), check_vma=False
    )
```

```python
import functools
import math

import jax
import jax.numpy as jnp
from jax import lax
from jax.experimental import pallas as pl
from jax.experimental.pallas import tpu as pltpu
from jax.sharding import PartitionSpec as P

RING = 4
HEADS = 8
HEAD = 128
BLK = 128
NB = 4
RADIUS = 7
ROWS = 64
HALF = NB // 2
PACKED = ROWS + 8
LOG2E = math.log2(math.e)
EXPONENT = LOG2E / math.sqrt(HEAD)
LOW = -1e30
MESH = pl.DeviceIdType.MESH
BF16, F32 = jnp.bfloat16, jnp.float32


def turn(value, steps):
    return lax.rem(value + (RING + steps), RING)


def kernel(
    width_ref, offset_ref, q_hbm, k_hbm, v_hbm, w_hbm, out_ref,
    k_0, k_1, k_2, k_3, v_0, v_1, v_2, v_3, q_all, w_all,
    peak_ref, total_ref, mixed_ref, packed, arrived, sums,
    local_sem, kv_send, kv_recv, q_send, q_recv, w_send, w_recv, o_send, o_recv, ready,
):
    frame, head = lax.axis_index("frame"), lax.axis_index("head")
    x, z = lax.div(frame, RING), lax.rem(frame, RING)
    y, core = lax.div(head, 2), lax.rem(head, 2)

    def at(x, z, head):
        return (x * RING + z, head)

    x_next, x_last = at(turn(x, 1), z, head), at(turn(x, -1), z, head)
    z_next, z_last = at(x, turn(z, 1), head), at(x, turn(z, -1), head)
    head_next, head_last = turn(y, 1) * 2 + core, turn(y, -1) * 2 + core
    head_far, head_pair = turn(y, 2) * 2 + core, y * 2 + 1 - core
    y_next, y_last, pair = at(x, z, head_next), at(x, z, head_last), at(x, z, head_pair)
    def remote(source, target, send, recv, device):
        return pltpu.make_async_remote_copy(
            src_ref=source, dst_ref=target, send_sem=send, recv_sem=recv,
            device_id=device, device_id_type=MESH,
        )

    barrier = pltpu.get_barrier_semaphore()
    greeted = [x_next, x_last, z_next, z_last, y_next, y_last, pair]
    for device in greeted:
        pl.semaphore_signal(barrier, inc=1, device_id=device, device_id_type=MESH)

    def announce(turn_, devices):
        for device in devices:
            pl.semaphore_signal(ready.at[turn_], inc=1, device_id=device, device_id_type=MESH)

    own = [
        pltpu.make_async_copy(q_hbm, q_all.at[0], local_sem.at[0]),
        pltpu.make_async_copy(k_hbm, k_0, local_sem.at[1]),
        pltpu.make_async_copy(v_hbm, v_0, local_sem.at[2]),
        pltpu.make_async_copy(w_hbm, w_all.at[head], local_sem.at[3]),
    ]
    for copy in own:
        copy.start()
    pl.semaphore_wait(barrier, len(greeted))

    kv = [
        remote(k_hbm, k_1, kv_send.at[0], kv_recv.at[0], x_next),
        remote(v_hbm, v_3, kv_send.at[1], kv_recv.at[1], x_last),
        remote(v_hbm, v_1, kv_send.at[2], kv_recv.at[2], x_next),
        remote(k_hbm, k_3, kv_send.at[3], kv_recv.at[3], x_last),
        remote(k_1, k_2, kv_send.at[4], kv_recv.at[4], x_next),
        remote(v_3, v_2, kv_send.at[5], kv_recv.at[5], x_last),
    ]
    low, high = pl.ds(0, HALF), pl.ds(HALF, HALF)
    qs = [
        remote(q_hbm.at[low], q_all.at[1, low], q_send.at[0], q_recv.at[0], z_next),
        remote(q_hbm.at[high], q_all.at[3, high], q_send.at[1], q_recv.at[1], z_last),
        remote(q_hbm.at[high], q_all.at[1, high], q_send.at[2], q_recv.at[2], z_next),
        remote(q_hbm.at[low], q_all.at[3, low], q_send.at[3], q_recv.at[3], z_last),
        remote(q_all.at[1, low], q_all.at[2, low], q_send.at[4], q_recv.at[4], z_next),
        remote(q_all.at[3, high], q_all.at[2, high], q_send.at[5], q_recv.at[5], z_last),
    ]
    part_rows = HEAD // RING

    def quarter(which, begin=0, size=part_rows):
        return pl.ds(pl.multiple_of(which * part_rows + begin, part_rows // 2), size)

    def weights(source, shard, rows, sem, device, send=None):
        return remote(
            source, w_all.at[shard, rows], w_send.at[sem if send is None else send], w_recv.at[sem], device
        )

    half_rows, later = part_rows // 2, HEAD - part_rows
    direct = [
        weights(w_hbm.at[quarter(turn(x, step))], head, quarter(turn(x, step)), side + min(step, 1), device)
        for step in range(RING) for side, device in ((0, y_next), (2, y_last))
    ]

    def passed(shard, which, begin, size, sem, device):
        rows = quarter(which, begin, size)
        return weights(w_all.at[shard, rows], shard, rows, sem, device)

    every_row = pl.ds(0, HEAD)
    ws = {
        4: passed(head_last, x, 0, half_rows, 4, y_next),
        5: passed(head_next, x, half_rows, half_rows, 5, y_last),
        6: passed(head_far, x, 0, part_rows, 6, x_next),
        7: passed(head_far, x, 0, part_rows, 7, x_last),
        8: passed(head_far, turn(x, -1), 0, half_rows, 8, x_next),
        9: passed(head_far, turn(x, 1), half_rows, half_rows, 9, x_last),
        10: weights(w_hbm, head, every_row, 10, pair),
        11: weights(w_all.at[head_last], head_last, every_row, 11, pair),
        12: weights(w_all.at[head_next], head_next, every_row, 12, pair),
        13: weights(w_all.at[head_far], head_far, every_row, 13, pair),
    }
    several = w_all.at[head, pl.ds(0, later)]
    for step in range(4):
        kv[step].start()
        qs[step].start()
    for copy in direct[:6]:
        copy.start()
    ws[10].start()
    announce(0, (z_next, z_last))

    ones = jnp.ones((BLK, HEAD), BF16)
    tokens = NB * BLK
    key_block = lax.broadcasted_iota(jnp.int32, (1, tokens), 1) // BLK

    def query_frame(slot):
        return x * RING + turn(z, -slot)

    def wide(slot, distance, k_ref, v_ref, valid):
        this = query_frame(slot)

        def pick(block):
            past = lax.rem(key_block + (NB - offset_ref[distance, block, this]), NB)
            inside = past < width_ref[distance, this]
            inside = inside | (key_block == jnp.where(distance == 0, block, NB))
            added = jnp.where(inside, 0.0, LOW)
            if valid is not None:
                added += jnp.where(valid, 0.0, LOW)
            return k_ref[...].reshape(tokens, HEAD), v_ref[...].reshape(tokens, HEAD), added

        return NB, pick

    def narrow(slot, distance, k_ref, v_ref, valid, count):
        this = query_frame(slot)

        def pick(block):
            offset = offset_ref[distance, block, this]
            chosen = [lax.rem(offset + step, NB) for step in range(count)]
            keys, values = [k_ref[index] for index in chosen], [v_ref[index] for index in chosen]
            if count > 1:
                keys, values = [jnp.concatenate(keys, axis=0)], [jnp.concatenate(values, axis=0)]
            return keys[0], values[0], None if valid is None else jnp.where(valid, 0.0, LOW)

        return count, pick

    def join(pieces):
        return pieces[0] if len(pieces) == 1 else jnp.concatenate(pieces, axis=0)

    def attend(slot, sources, first, blocks):
        count = sum(source[0] for source in sources)
        states, scores, values = [], [], []
        for block in blocks:
            picked = [source[1](block) for source in sources]
            full = lax.dot_general(
                q_all[slot, block], join([keys for keys, _, _ in picked]), (((1,), (1,)), ((), ())),
                preferred_element_type=F32,
            )
            parts = [full[:, step * BLK:(step + 1) * BLK] for step in range(count)]
            begin = 0
            for (size, _), (_, _, added) in zip(sources, picked):
                for step in range(size):
                    if added is not None:
                        more = added[:, step * BLK:(step + 1) * BLK] if added.ndim else added
                        parts[begin + step] += more
                begin += size
            scores.append(parts)
            values.append(join([rows for _, rows, _ in picked]))
        keeps, peaks = [], []
        for block, parts in zip(blocks, scores):
            peak = jnp.max(functools.reduce(jnp.maximum, parts), axis=1, keepdims=True)
            if not first:
                before = peak_ref[slot, block]
                peak = jnp.maximum(before, peak)
                keeps.append(jnp.exp2((before - peak) * EXPONENT))
            peaks.append(peak)
        updates = []
        for parts, peak, rows in zip(scores, peaks, values):
            weights = [jnp.exp2((part - peak) * EXPONENT).astype(BF16) for part in parts]
            weights = weights[0] if count == 1 else jnp.concatenate(weights, axis=1)
            extended = jnp.concatenate([rows, join([ones] * count)], axis=1)
            updates.append(jnp.dot(weights, extended, preferred_element_type=F32))
        for index, block in enumerate(blocks):
            mixed, total = updates[index][:, :HEAD], updates[index][:, HEAD:]
            if not first:
                mixed += mixed_ref[slot, block] * keeps[index]
                total += total_ref[slot, block] * keeps[index]
            states.append((jnp.broadcast_to(peaks[index], (BLK, HEAD)), total, mixed))
        return states

    def keep(slot, states, blocks):
        for block, (peak, total, mixed) in zip(blocks, states):
            peak_ref[slot, block] = peak
            total_ref[slot, block] = total
            mixed_ref[slot, block] = mixed

    def absorb(slot, sources, first, group):
        for begin in range(0, NB, group):
            blocks = range(begin, begin + group)
            keep(slot, attend(slot, sources, first, blocks), blocks)

    row = lax.broadcasted_iota(jnp.int32, (BLK, BLK), 0)
    lane = lax.broadcasted_iota(jnp.int32, (BLK, BLK), 1)
    small_row = lax.broadcasted_iota(jnp.int32, (8, BLK), 0)

    def pack(slot, states):
        for block, (peak, total, mixed) in enumerate(states):
            scaled = (mixed / total).astype(BF16)
            level = peak * EXPONENT + jnp.log(total) * LOG2E
            level = jnp.sum(jnp.where(row == lane, level, 0.0), axis=0, keepdims=True)
            first = level.astype(BF16).astype(F32)
            second = (level - first).astype(BF16).astype(F32)
            tile = jnp.where(
                small_row == 0, first,
                jnp.where(small_row == 1, second, jnp.where(small_row == 2, level - first - second, 0.0)),
            ).astype(BF16)
            for half in range(2):
                packed[slot, 2 * block + half, 0:ROWS, :] = scaled[half * ROWS:(half + 1) * ROWS]
                packed[slot, 2 * block + half, ROWS:PACKED, :] = tile

    def send(slot):
        def each(step, carry):
            receiver = lax.rem(2 * y + RING + step, HEADS)
            source, target = packed.at[slot, receiver], arrived.at[head, z]
            here = (slot == 0) & (receiver == head)

            @pl.when(here)
            def _():
                pltpu.make_async_copy(source, target, local_sem.at[4]).start()

            @pl.when(jnp.logical_not(here))
            def _():
                remote(
                    source, target, o_send.at[slot], o_recv.at[head], at(x, turn(z, -slot), receiver)
                ).start()

            return carry

        lax.fori_loop(0, HEADS, each, 0)

    every = range(NB)
    qs[0].wait_recv()
    qs[4].start()
    qs[1].wait_recv()
    qs[5].start()
    for copy in own[:3]:
        copy.wait()
    pl.semaphore_wait(ready.at[0], 2)
    announce(1, (y_next, y_last))

    def own_keys(step, carry):
        slot = step + lax.div(step, 2) - 2 * lax.div(step, 3)

        @pl.when(step == 1)
        def _():
            kv[0].wait_recv()
            kv[4].start()
            kv[1].wait_recv()
            kv[5].start()
            qs[2].wait_recv()
            qs[3].wait_recv()
            direct[0].wait_recv()
            ws[4].start()
            direct[1].wait_recv()
            ws[5].start()
            for copy in direct[6:]:
                copy.start()
            pl.semaphore_wait(ready.at[1], 2)
            announce(2, (y_next, y_last))

        @pl.when(step == 3)
        def _():
            qs[4].wait_recv()
            qs[5].wait_recv()
            pl.semaphore_wait(ready.at[2], 2)
            announce(3, (pair,))

        ahead = turn(z, -slot) - z
        distance = jnp.maximum(ahead, -ahead)

        @pl.when(distance <= 1)
        def _():
            absorb(slot, [wide(slot, distance, k_0, v_0, None)], True, 2)

        @pl.when(distance >= 2)
        def _():
            absorb(slot, [narrow(slot, distance, k_0, v_0, None, 2)], True, NB)

        return carry

    lax.fori_loop(0, RING, own_keys, 0)
    kv[2].wait_recv()
    kv[3].wait_recv()

    def near_keys(slot, carry):
        ahead = turn(z, -slot) - z
        distance = jnp.maximum(ahead, -ahead)
        last, next_ = (k_1, v_1, x >= 1), (k_3, v_3, x <= RING - 2)

        @pl.when(distance == 0)
        def _():
            absorb(slot, [narrow(slot, RING, *last, 1), narrow(slot, RING, *next_, 1)], False, NB)

        for sign, near, far in ((1, next_, last), (-1, last, next_)):

            @pl.when((ahead * sign >= 1) & (ahead * sign <= 2))
            def _():
                absorb(
                    slot,
                    [
                        narrow(slot, RING - distance, *near, 2),
                        narrow(slot, RING + distance, *far, 1),
                    ],
                    False, NB,
                )

            @pl.when(ahead * sign == 3)
            def _():
                absorb(slot, [wide(slot, 1, *near), narrow(slot, RADIUS, *far, 1)], False, 2)

        return carry

    lax.fori_loop(0, RING, near_keys, 0)

    ws[4].wait_recv()
    ws[5].wait_recv()
    ws[6].start()
    ws[7].start()
    pl.semaphore_wait(ready.at[3], 1)
    far_frame = turn(x, 2) * RING + z

    def far_keys(slot):
        this = query_frame(slot)
        distance = jnp.maximum(this - far_frame, far_frame - this)
        source = narrow(slot, jnp.minimum(distance, RADIUS), k_2, v_2, distance <= RADIUS, 1)
        return attend(slot, [source], False, every)

    pack(0, [(peak_ref[0, b], total_ref[0, b], mixed_ref[0, b]) for b in every])
    send(0)
    kv[4].wait_recv()
    kv[5].wait_recv()
    pack(2, far_keys(2))
    send(2)
    states = far_keys(3), far_keys(1)
    pack(3, states[0])
    pack(1, states[1])
    send(3)
    send(1)
    ws[6].wait_recv()
    ws[8].start()
    ws[7].wait_recv()
    ws[9].start()
    pltpu.make_async_copy(several, several, w_recv.at[1]).wait()
    ws[11].start()
    pltpu.make_async_copy(several, several, w_recv.at[3]).wait()
    ws[12].start()
    ws[8].wait_recv()
    ws[9].wait_recv()
    ws[13].start()

    column = lax.broadcasted_iota(jnp.int32, (ROWS, HEAD), 1)
    here = lax.broadcasted_iota(jnp.int32, (ROWS, HEAD), 0) + core * ROWS

    def merge(other):
        levels = []
        for part in range(RING):
            tile = arrived[other, part, ROWS:PACKED, :].astype(F32)
            levels.append(jnp.sum(tile, axis=0, keepdims=True))
        peak = functools.reduce(jnp.maximum, levels)
        shares = [jnp.exp2(level - peak) for level in levels]
        whole = functools.reduce(jnp.add, shares)
        merged = jnp.zeros((ROWS, HEAD), F32)
        for part in range(RING):
            share = jnp.broadcast_to(shares[part] / whole, (ROWS, HEAD))
            share = jnp.sum(jnp.where(column == here, share, 0.0), axis=1, keepdims=True)
            merged += arrived[other, part, 0:ROWS, :].astype(F32) * share
        return merged.astype(BF16)

    pltpu.make_async_copy(packed.at[0, head], arrived.at[head, z], local_sem.at[4]).wait()
    own[3].wait()
    for step in range(10, 13):
        ws[step].wait_recv()

    columns, tile = w_all.shape[2], 512
    for index, step in enumerate((0, -1, 1, 2)):
        chip = turn(y, step)
        if step == 2:
            ws[13].wait_recv()
        for side in range(2):
            other = chip * 2 + side

            @pl.when(other == head)
            def _():
                three = arrived.at[other, pl.ds(0, RING - 1)]
                pltpu.make_async_copy(three, three, o_recv.at[other]).wait()

            @pl.when(other != head)
            def _():
                pltpu.make_async_copy(arrived.at[other], arrived.at[other], o_recv.at[other]).wait()

        left = jnp.concatenate([merge(chip * 2), merge(chip * 2 + 1)], axis=1)
        for start in range(0, columns, tile):
            weight = w_all[pl.ds(chip * 2, 2), :, start:start + tile].reshape(2 * HEAD, tile)
            term = jnp.dot(left, weight, preferred_element_type=F32)
            if index > 0:
                term += sums[:, start:start + tile]
            if index < RING - 1:
                sums[:, start:start + tile] = term
            else:
                out_ref[:, start:start + tile] = term

    for copy in kv + qs + direct[:2] + list(ws.values()):
        copy.wait_send()
    for sem in (1, 3):
        pltpu.make_async_copy(several, several, w_send.at[sem]).wait()
    seven = packed.at[0, pl.ds(0, HEADS - 1)]
    pltpu.make_async_copy(seven, seven, o_send.at[0]).wait()
    for slot in range(1, RING):
        pltpu.make_async_copy(packed.at[slot], packed.at[slot], o_send.at[slot]).wait()


def on_device(queries, keys, values, band_width, band_offset, out_weight):
    width = out_weight.shape[1]
    queries, keys, values = (array.reshape(NB, BLK, HEAD) for array in (queries, keys, values))
    band_width, band_offset = band_width.T, band_offset.transpose(1, 2, 0)
    band_width, band_offset, queries, keys, values, out_weight = (
        pltpu.with_memory_space_constraint(array, pltpu.HBM)
        for array in (band_width, band_offset, queries, keys, values, out_weight)
    )
    block = pltpu.VMEM((NB, BLK, HEAD), BF16)
    state = pltpu.VMEM((RING, NB, BLK, HEAD), F32)
    dma = pltpu.SemaphoreType.DMA
    smem, anywhere = pl.BlockSpec(memory_space=pltpu.SMEM), pl.BlockSpec(memory_space=pltpu.HBM)
    return pl.pallas_call(
        kernel,
        out_shape=jax.ShapeDtypeStruct((ROWS, width), F32),
        in_specs=[smem, smem] + [anywhere] * 4,
        out_specs=pl.BlockSpec(memory_space=pltpu.VMEM),
        scratch_shapes=[block] * 8
        + [
            pltpu.VMEM((RING, NB, BLK, HEAD), BF16),
            pltpu.VMEM((HEADS, HEAD, width), BF16),
            state, state, state,
            pltpu.VMEM((RING, HEADS, PACKED, HEAD), BF16),
            pltpu.VMEM((HEADS, RING, PACKED, HEAD), BF16),
            pltpu.VMEM((ROWS, width), F32),
            dma((5,)), dma((6,)), dma((6,)), dma((6,)), dma((6,)), dma((14,)), dma((14,)),
            dma((RING,)), dma((HEADS,)), pltpu.SemaphoreType.REGULAR((4,)),
        ],
        compiler_params=pltpu.CompilerParams(
            collective_id=0, has_side_effects=True, vmem_limit_bytes=52 * 1024 * 1024
        ),
    )(band_width, band_offset, queries, keys, values, out_weight).astype(BF16)


def solution(mesh):
    placed = (P("frame", "head"), P("frame", "head"), P("frame", "head"), P(), P(), P("head", None))
    return jax.shard_map(
        on_device, mesh=mesh, in_specs=placed, out_specs=P(("frame", "head"), None), check_vma=False
    )
```

```python
import functools
import math

import jax
import jax.numpy as jnp
from jax import lax
from jax.experimental import pallas as pl
from jax.experimental.pallas import tpu as pltpu
from jax.sharding import PartitionSpec as P

RING = 4
HEADS = 8
HEAD = 128
BLK = 128
NB = 4
RADIUS = 7
ROWS = 64
HALF = NB // 2
PACKED = ROWS + 8
LOG2E = math.log2(math.e)
EXPONENT = LOG2E / math.sqrt(HEAD)
LOW = -1e30
MESH = pl.DeviceIdType.MESH
BF16, F32 = jnp.bfloat16, jnp.float32


def turn(value, steps):
    return lax.rem(value + (RING + steps), RING)


def kernel(
    width_hbm, offset_hbm, q_hbm, k_hbm, v_hbm, w_hbm, out_ref,
    width_ref, offset_ref, k_0, k_1, k_2, k_3, v_0, v_1, v_2, v_3, q_all, w_all,
    peak_ref, total_ref, mixed_ref, packed, arrived, sums,
    local_sem, kv_send, kv_recv, q_send, q_recv, w_send, w_recv, o_send, o_recv, ready,
):
    frame, head = lax.axis_index("frame"), lax.axis_index("head")
    x, z = lax.div(frame, RING), lax.rem(frame, RING)
    y, core = lax.div(head, 2), lax.rem(head, 2)

    def at(x, z, head):
        return (x * RING + z, head)

    x_next, x_last = at(turn(x, 1), z, head), at(turn(x, -1), z, head)
    z_next, z_last = at(x, turn(z, 1), head), at(x, turn(z, -1), head)
    head_next, head_last = turn(y, 1) * 2 + core, turn(y, -1) * 2 + core
    head_far, head_pair = turn(y, 2) * 2 + core, y * 2 + 1 - core
    y_next, y_last, pair = at(x, z, head_next), at(x, z, head_last), at(x, z, head_pair)
    def remote(source, target, send, recv, device):
        return pltpu.make_async_remote_copy(
            src_ref=source, dst_ref=target, send_sem=send, recv_sem=recv,
            device_id=device, device_id_type=MESH,
        )

    barrier = pltpu.get_barrier_semaphore()
    greeted = [x_next, x_last, z_next, z_last, y_next, y_last, pair]
    for device in greeted:
        pl.semaphore_signal(barrier, inc=1, device_id=device, device_id_type=MESH)

    def announce(turn_, devices):
        for device in devices:
            pl.semaphore_signal(ready.at[turn_], inc=1, device_id=device, device_id_type=MESH)

    own = [
        pltpu.make_async_copy(q_hbm, q_all.at[0], local_sem.at[0]),
        pltpu.make_async_copy(k_hbm, k_0, local_sem.at[1]),
        pltpu.make_async_copy(v_hbm, v_0, local_sem.at[2]),
        pltpu.make_async_copy(w_hbm, w_all.at[head], local_sem.at[3]),
        pltpu.make_async_copy(width_hbm, width_ref, local_sem.at[5]),
        pltpu.make_async_copy(offset_hbm, offset_ref, local_sem.at[6]),
    ]
    for copy in own:
        copy.start()
    pl.semaphore_wait(barrier, len(greeted))

    kv = [
        remote(k_hbm, k_1, kv_send.at[0], kv_recv.at[0], x_next),
        remote(v_hbm, v_3, kv_send.at[1], kv_recv.at[1], x_last),
        remote(v_hbm, v_1, kv_send.at[2], kv_recv.at[2], x_next),
        remote(k_hbm, k_3, kv_send.at[3], kv_recv.at[3], x_last),
        remote(k_1, k_2, kv_send.at[4], kv_recv.at[4], x_next),
        remote(v_3, v_2, kv_send.at[5], kv_recv.at[5], x_last),
    ]
    low, high = pl.ds(0, HALF), pl.ds(HALF, HALF)
    qs = [
        remote(q_hbm.at[low], q_all.at[1, low], q_send.at[0], q_recv.at[0], z_next),
        remote(q_hbm.at[high], q_all.at[3, high], q_send.at[1], q_recv.at[1], z_last),
        remote(q_hbm.at[high], q_all.at[1, high], q_send.at[2], q_recv.at[2], z_next),
        remote(q_hbm.at[low], q_all.at[3, low], q_send.at[3], q_recv.at[3], z_last),
        remote(q_all.at[1, low], q_all.at[2, low], q_send.at[4], q_recv.at[4], z_next),
        remote(q_all.at[3, high], q_all.at[2, high], q_send.at[5], q_recv.at[5], z_last),
    ]
    part_rows = HEAD // RING

    def quarter(which, begin=0, size=part_rows):
        return pl.ds(pl.multiple_of(which * part_rows + begin, part_rows // 2), size)

    def weights(source, shard, rows, sem, device, send=None):
        return remote(
            source, w_all.at[shard, rows], w_send.at[sem if send is None else send], w_recv.at[sem], device
        )

    half_rows, later = part_rows // 2, HEAD - part_rows
    direct = [
        weights(w_hbm.at[quarter(turn(x, step))], head, quarter(turn(x, step)), side + min(step, 1), device)
        for step in range(RING) for side, device in ((0, y_next), (2, y_last))
    ]

    def passed(shard, which, begin, size, sem, device):
        rows = quarter(which, begin, size)
        return weights(w_all.at[shard, rows], shard, rows, sem, device)

    every_row = pl.ds(0, HEAD)
    ws = {
        4: passed(head_last, x, 0, half_rows, 4, y_next),
        5: passed(head_next, x, half_rows, half_rows, 5, y_last),
        6: passed(head_far, x, 0, part_rows, 6, x_next),
        7: passed(head_far, x, 0, part_rows, 7, x_last),
        8: passed(head_far, turn(x, -1), 0, half_rows, 8, x_next),
        9: passed(head_far, turn(x, 1), half_rows, half_rows, 9, x_last),
        10: weights(w_hbm, head, every_row, 10, pair),
        11: weights(w_all.at[head_last], head_last, every_row, 11, pair),
        12: weights(w_all.at[head_next], head_next, every_row, 12, pair),
        13: weights(w_all.at[head_far], head_far, every_row, 13, pair),
    }
    several = w_all.at[head, pl.ds(0, later)]
    for step in range(4):
        kv[step].start()
        qs[step].start()
    for copy in direct[:6]:
        copy.start()
    ws[10].start()
    announce(0, (z_next, z_last))

    ones = jnp.ones((BLK, HEAD), BF16)
    tokens = NB * BLK
    key_block = lax.broadcasted_iota(jnp.int32, (1, tokens), 1) // BLK

    def query_frame(slot):
        return x * RING + turn(z, -slot)

    def wide(slot, distance, k_ref, v_ref, valid):
        this = query_frame(slot)

        def pick(block):
            past = lax.rem(key_block + (NB - offset_ref[distance, block, this]), NB)
            inside = past < width_ref[distance, this]
            inside = inside | (key_block == jnp.where(distance == 0, block, NB))
            added = jnp.where(inside, 0.0, LOW)
            if valid is not None:
                added += jnp.where(valid, 0.0, LOW)
            return k_ref[...].reshape(tokens, HEAD), v_ref[...].reshape(tokens, HEAD), added

        return NB, pick

    def narrow(slot, distance, k_ref, v_ref, valid, count):
        this = query_frame(slot)

        def pick(block):
            offset = offset_ref[distance, block, this]
            chosen = [lax.rem(offset + step, NB) for step in range(count)]
            keys, values = [k_ref[index] for index in chosen], [v_ref[index] for index in chosen]
            if count > 1:
                keys, values = [jnp.concatenate(keys, axis=0)], [jnp.concatenate(values, axis=0)]
            return keys[0], values[0], None if valid is None else jnp.where(valid, 0.0, LOW)

        return count, pick

    def join(pieces):
        return pieces[0] if len(pieces) == 1 else jnp.concatenate(pieces, axis=0)

    def attend(slot, sources, first, blocks):
        count = sum(source[0] for source in sources)
        states, scores, values = [], [], []
        for block in blocks:
            picked = [source[1](block) for source in sources]
            full = lax.dot_general(
                q_all[slot, block], join([keys for keys, _, _ in picked]), (((1,), (1,)), ((), ())),
                preferred_element_type=F32,
            )
            parts = [full[:, step * BLK:(step + 1) * BLK] for step in range(count)]
            begin = 0
            for (size, _), (_, _, added) in zip(sources, picked):
                for step in range(size):
                    if added is not None:
                        more = added[:, step * BLK:(step + 1) * BLK] if added.ndim else added
                        parts[begin + step] += more
                begin += size
            scores.append(parts)
            values.append(join([rows for _, rows, _ in picked]))
        keeps, peaks = [], []
        for block, parts in zip(blocks, scores):
            peak = jnp.max(functools.reduce(jnp.maximum, parts), axis=1, keepdims=True)
            if not first:
                before = peak_ref[slot, block]
                peak = jnp.maximum(before, peak)
                keeps.append(jnp.exp2((before - peak) * EXPONENT))
            peaks.append(peak)
        updates = []
        for parts, peak, rows in zip(scores, peaks, values):
            weights = [jnp.exp2((part - peak) * EXPONENT).astype(BF16) for part in parts]
            weights = weights[0] if count == 1 else jnp.concatenate(weights, axis=1)
            extended = jnp.concatenate([rows, join([ones] * count)], axis=1)
            updates.append(jnp.dot(weights, extended, preferred_element_type=F32))
        for index, block in enumerate(blocks):
            mixed, total = updates[index][:, :HEAD], updates[index][:, HEAD:]
            if not first:
                mixed += mixed_ref[slot, block] * keeps[index]
                total += total_ref[slot, block] * keeps[index]
            states.append((jnp.broadcast_to(peaks[index], (BLK, HEAD)), total, mixed))
        return states

    def keep(slot, states, blocks):
        for block, (peak, total, mixed) in zip(blocks, states):
            peak_ref[slot, block] = peak
            total_ref[slot, block] = total
            mixed_ref[slot, block] = mixed

    def absorb(slot, sources, first, group):
        for begin in range(0, NB, group):
            blocks = range(begin, begin + group)
            keep(slot, attend(slot, sources, first, blocks), blocks)

    row = lax.broadcasted_iota(jnp.int32, (BLK, BLK), 0)
    lane = lax.broadcasted_iota(jnp.int32, (BLK, BLK), 1)
    small_row = lax.broadcasted_iota(jnp.int32, (8, BLK), 0)

    def pack(slot, states):
        for block, (peak, total, mixed) in enumerate(states):
            scaled = (mixed / total).astype(BF16)
            level = peak * EXPONENT + jnp.log(total) * LOG2E
            level = jnp.sum(jnp.where(row == lane, level, 0.0), axis=0, keepdims=True)
            first = level.astype(BF16).astype(F32)
            second = (level - first).astype(BF16).astype(F32)
            tile = jnp.where(
                small_row == 0, first,
                jnp.where(small_row == 1, second, jnp.where(small_row == 2, level - first - second, 0.0)),
            ).astype(BF16)
            for half in range(2):
                packed[slot, 2 * block + half, 0:ROWS, :] = scaled[half * ROWS:(half + 1) * ROWS]
                packed[slot, 2 * block + half, ROWS:PACKED, :] = tile

    def send(slot):
        def each(step, carry):
            receiver = lax.rem(2 * y + RING + step, HEADS)
            source, target = packed.at[slot, receiver], arrived.at[head, z]
            here = (slot == 0) & (receiver == head)

            @pl.when(here)
            def _():
                pltpu.make_async_copy(source, target, local_sem.at[4]).start()

            @pl.when(jnp.logical_not(here))
            def _():
                remote(
                    source, target, o_send.at[slot], o_recv.at[head], at(x, turn(z, -slot), receiver)
                ).start()

            return carry

        lax.fori_loop(0, HEADS, each, 0)

    every = range(NB)
    qs[0].wait_recv()
    qs[4].start()
    qs[1].wait_recv()
    qs[5].start()
    for copy in own[:3] + own[4:]:
        copy.wait()
    pl.semaphore_wait(ready.at[0], 2)
    announce(1, (y_next, y_last))

    def own_keys(step, carry):
        slot = step + lax.div(step, 2) - 2 * lax.div(step, 3)

        @pl.when(step == 1)
        def _():
            kv[0].wait_recv()
            kv[4].start()
            kv[1].wait_recv()
            kv[5].start()
            qs[2].wait_recv()
            qs[3].wait_recv()
            direct[0].wait_recv()
            ws[4].start()
            direct[1].wait_recv()
            ws[5].start()
            for copy in direct[6:]:
                copy.start()
            pl.semaphore_wait(ready.at[1], 2)
            announce(2, (y_next, y_last))

        @pl.when(step == 3)
        def _():
            qs[4].wait_recv()
            qs[5].wait_recv()
            pl.semaphore_wait(ready.at[2], 2)
            announce(3, (pair,))

        ahead = turn(z, -slot) - z
        distance = jnp.maximum(ahead, -ahead)

        @pl.when(distance <= 1)
        def _():
            absorb(slot, [wide(slot, distance, k_0, v_0, None)], True, 2)

        @pl.when(distance >= 2)
        def _():
            absorb(slot, [narrow(slot, distance, k_0, v_0, None, 2)], True, NB)

        return carry

    lax.fori_loop(0, RING, own_keys, 0)
    kv[2].wait_recv()
    kv[3].wait_recv()

    def near_keys(slot, carry):
        ahead = turn(z, -slot) - z
        distance = jnp.maximum(ahead, -ahead)
        last, next_ = (k_1, v_1, x >= 1), (k_3, v_3, x <= RING - 2)

        @pl.when(distance == 0)
        def _():
            absorb(slot, [narrow(slot, RING, *last, 1), narrow(slot, RING, *next_, 1)], False, NB)

        for sign, near, far in ((1, next_, last), (-1, last, next_)):

            @pl.when((ahead * sign >= 1) & (ahead * sign <= 2))
            def _():
                absorb(
                    slot,
                    [
                        narrow(slot, RING - distance, *near, 2),
                        narrow(slot, RING + distance, *far, 1),
                    ],
                    False, NB,
                )

            @pl.when(ahead * sign == 3)
            def _():
                absorb(slot, [wide(slot, 1, *near), narrow(slot, RADIUS, *far, 1)], False, 2)

        return carry

    lax.fori_loop(0, RING, near_keys, 0)

    ws[4].wait_recv()
    ws[5].wait_recv()
    ws[6].start()
    ws[7].start()
    pl.semaphore_wait(ready.at[3], 1)
    far_frame = turn(x, 2) * RING + z

    def far_keys(slot):
        this = query_frame(slot)
        distance = jnp.maximum(this - far_frame, far_frame - this)
        source = narrow(slot, jnp.minimum(distance, RADIUS), k_2, v_2, distance <= RADIUS, 1)
        return attend(slot, [source], False, every)

    pack(0, [(peak_ref[0, b], total_ref[0, b], mixed_ref[0, b]) for b in every])
    send(0)
    kv[4].wait_recv()
    kv[5].wait_recv()
    pack(2, far_keys(2))
    send(2)
    states = far_keys(3), far_keys(1)
    pack(3, states[0])
    pack(1, states[1])
    send(3)
    send(1)
    ws[6].wait_recv()
    ws[8].start()
    ws[7].wait_recv()
    ws[9].start()
    pltpu.make_async_copy(several, several, w_recv.at[1]).wait()
    ws[11].start()
    pltpu.make_async_copy(several, several, w_recv.at[3]).wait()
    ws[12].start()
    ws[8].wait_recv()
    ws[9].wait_recv()
    ws[13].start()

    column = lax.broadcasted_iota(jnp.int32, (ROWS, HEAD), 1)
    here = lax.broadcasted_iota(jnp.int32, (ROWS, HEAD), 0) + core * ROWS

    def merge(other):
        levels = []
        for part in range(RING):
            tile = arrived[other, part, ROWS:PACKED, :].astype(F32)
            levels.append(jnp.sum(tile, axis=0, keepdims=True))
        peak = functools.reduce(jnp.maximum, levels)
        shares = [jnp.exp2(level - peak) for level in levels]
        whole = functools.reduce(jnp.add, shares)
        merged = jnp.zeros((ROWS, HEAD), F32)
        for part in range(RING):
            share = jnp.broadcast_to(shares[part] / whole, (ROWS, HEAD))
            share = jnp.sum(jnp.where(column == here, share, 0.0), axis=1, keepdims=True)
            merged += arrived[other, part, 0:ROWS, :].astype(F32) * share
        return merged.astype(BF16)

    pltpu.make_async_copy(packed.at[0, head], arrived.at[head, z], local_sem.at[4]).wait()
    own[3].wait()
    for step in range(10, 13):
        ws[step].wait_recv()

    columns, tile = w_all.shape[2], 512
    for index, step in enumerate((0, -1, 1, 2)):
        chip = turn(y, step)
        if step == 2:
            ws[13].wait_recv()
        for side in range(2):
            other = chip * 2 + side

            @pl.when(other == head)
            def _():
                three = arrived.at[other, pl.ds(0, RING - 1)]
                pltpu.make_async_copy(three, three, o_recv.at[other]).wait()

            @pl.when(other != head)
            def _():
                pltpu.make_async_copy(arrived.at[other], arrived.at[other], o_recv.at[other]).wait()

        left = jnp.concatenate([merge(chip * 2), merge(chip * 2 + 1)], axis=1)
        for start in range(0, columns, tile):
            weight = w_all[pl.ds(chip * 2, 2), :, start:start + tile].reshape(2 * HEAD, tile)
            term = jnp.dot(left, weight, preferred_element_type=F32)
            if index > 0:
                term += sums[:, start:start + tile]
            if index < RING - 1:
                sums[:, start:start + tile] = term
            else:
                out_ref[:, start:start + tile] = term

    for copy in kv + qs + direct[:2] + list(ws.values()):
        copy.wait_send()
    for sem in (1, 3):
        pltpu.make_async_copy(several, several, w_send.at[sem]).wait()
    seven = packed.at[0, pl.ds(0, HEADS - 1)]
    pltpu.make_async_copy(seven, seven, o_send.at[0]).wait()
    for slot in range(1, RING):
        pltpu.make_async_copy(packed.at[slot], packed.at[slot], o_send.at[slot]).wait()


def on_device(queries, keys, values, band_width, band_offset, out_weight):
    width = out_weight.shape[1]
    queries, keys, values = (array.reshape(NB, BLK, HEAD) for array in (queries, keys, values))
    band_width, band_offset = band_width.T, band_offset.transpose(1, 2, 0)
    band_width, band_offset, queries, keys, values, out_weight = (
        pltpu.with_memory_space_constraint(array, pltpu.HBM)
        for array in (band_width, band_offset, queries, keys, values, out_weight)
    )
    block = pltpu.VMEM((NB, BLK, HEAD), BF16)
    state = pltpu.VMEM((RING, NB, BLK, HEAD), F32)
    dma = pltpu.SemaphoreType.DMA
    anywhere = pl.BlockSpec(memory_space=pltpu.HBM)
    return pl.pallas_call(
        kernel,
        out_shape=jax.ShapeDtypeStruct((ROWS, width), F32),
        in_specs=[anywhere] * 6,
        out_specs=pl.BlockSpec(memory_space=pltpu.VMEM),
        scratch_shapes=[pltpu.SMEM(band_width.shape, jnp.int32), pltpu.SMEM(band_offset.shape, jnp.int32)]
        + [block] * 8
        + [
            pltpu.VMEM((RING, NB, BLK, HEAD), BF16),
            pltpu.VMEM((HEADS, HEAD, width), BF16),
            state, state, state,
            pltpu.VMEM((RING, HEADS, PACKED, HEAD), BF16),
            pltpu.VMEM((HEADS, RING, PACKED, HEAD), BF16),
            pltpu.VMEM((ROWS, width), F32),
            dma((7,)), dma((6,)), dma((6,)), dma((6,)), dma((6,)), dma((14,)), dma((14,)),
            dma((RING,)), dma((HEADS,)), pltpu.SemaphoreType.REGULAR((4,)),
        ],
        compiler_params=pltpu.CompilerParams(
            collective_id=0, has_side_effects=True, vmem_limit_bytes=52 * 1024 * 1024
        ),
    )(band_width, band_offset, queries, keys, values, out_weight).astype(BF16)


def solution(mesh):
    placed = (P("frame", "head"), P("frame", "head"), P("frame", "head"), P(), P(), P("head", None))
    return jax.shard_map(
        on_device, mesh=mesh, in_specs=placed, out_specs=P(("frame", "head"), None), check_vma=False
    )
```

```python
import functools
import math

import jax
import jax.numpy as jnp
from jax import lax
from jax.experimental import pallas as pl
from jax.experimental.pallas import tpu as pltpu
from jax.sharding import PartitionSpec as P

RING = 4
HEADS = 8
HEAD = 128
BLK = 128
NB = 4
RADIUS = 7
ROWS = 64
HALF = NB // 2
PACKED = ROWS + 8
LOG2E = math.log2(math.e)
EXPONENT = LOG2E / math.sqrt(HEAD)
LOW = -1e30
MESH = pl.DeviceIdType.MESH
BF16, F32 = jnp.bfloat16, jnp.float32


def turn(value, steps):
    return lax.rem(value + (RING + steps), RING)


def kernel(
    width_hbm, offset_hbm, q_hbm, k_hbm, v_hbm, w_hbm, out_ref,
    width_ref, offset_ref, k_0, k_1, k_2, k_3, v_0, v_1, v_2, v_3, q_all, w_all,
    peak_ref, total_ref, mixed_ref, packed, arrived, sums,
    local_sem, kv_send, kv_recv, q_send, q_recv, w_send, w_recv, o_send, o_recv, ready,
):
    frame, head = lax.axis_index("frame"), lax.axis_index("head")
    x, z = lax.div(frame, RING), lax.rem(frame, RING)
    y, core = lax.div(head, 2), lax.rem(head, 2)

    def at(x, z, head):
        return (x * RING + z, head)

    x_next, x_last = at(turn(x, 1), z, head), at(turn(x, -1), z, head)
    z_next, z_last = at(x, turn(z, 1), head), at(x, turn(z, -1), head)
    head_next, head_last = turn(y, 1) * 2 + core, turn(y, -1) * 2 + core
    head_far, head_pair = turn(y, 2) * 2 + core, y * 2 + 1 - core
    y_next, y_last, pair = at(x, z, head_next), at(x, z, head_last), at(x, z, head_pair)
    def remote(source, target, send, recv, device):
        return pltpu.make_async_remote_copy(
            src_ref=source, dst_ref=target, send_sem=send, recv_sem=recv,
            device_id=device, device_id_type=MESH,
        )

    barrier = pltpu.get_barrier_semaphore()
    greeted = [x_next, x_last, z_next, z_last, y_next, y_last, pair]
    for device in greeted:
        pl.semaphore_signal(barrier, inc=1, device_id=device, device_id_type=MESH)

    def announce(turn_, devices):
        for device in devices:
            pl.semaphore_signal(ready.at[turn_], inc=1, device_id=device, device_id_type=MESH)

    own = [
        pltpu.make_async_copy(q_hbm, q_all.at[0], local_sem.at[0]),
        pltpu.make_async_copy(k_hbm, k_0, local_sem.at[1]),
        pltpu.make_async_copy(v_hbm, v_0, local_sem.at[2]),
        pltpu.make_async_copy(w_hbm, w_all.at[head], local_sem.at[3]),
        pltpu.make_async_copy(width_hbm, width_ref, local_sem.at[5]),
        pltpu.make_async_copy(offset_hbm, offset_ref, local_sem.at[6]),
    ]
    for copy in own:
        copy.start()
    pl.semaphore_wait(barrier, len(greeted))

    kv = [
        remote(k_hbm, k_1, kv_send.at[0], kv_recv.at[0], x_next),
        remote(v_hbm, v_3, kv_send.at[1], kv_recv.at[1], x_last),
        remote(v_hbm, v_1, kv_send.at[2], kv_recv.at[2], x_next),
        remote(k_hbm, k_3, kv_send.at[3], kv_recv.at[3], x_last),
        remote(k_1, k_2, kv_send.at[4], kv_recv.at[4], x_next),
        remote(v_3, v_2, kv_send.at[5], kv_recv.at[5], x_last),
    ]
    low, high = pl.ds(0, HALF), pl.ds(HALF, HALF)
    qs = [
        remote(q_hbm.at[low], q_all.at[1, low], q_send.at[0], q_recv.at[0], z_next),
        remote(q_hbm.at[high], q_all.at[3, high], q_send.at[1], q_recv.at[1], z_last),
        remote(q_hbm.at[high], q_all.at[1, high], q_send.at[2], q_recv.at[2], z_next),
        remote(q_hbm.at[low], q_all.at[3, low], q_send.at[3], q_recv.at[3], z_last),
        remote(q_all.at[1, low], q_all.at[2, low], q_send.at[4], q_recv.at[4], z_next),
        remote(q_all.at[3, high], q_all.at[2, high], q_send.at[5], q_recv.at[5], z_last),
    ]
    part_rows = HEAD // RING

    def quarter(which, begin=0, size=part_rows):
        return pl.ds(pl.multiple_of(which * part_rows + begin, part_rows // 2), size)

    def weights(source, shard, rows, sem, device, send=None):
        return remote(
            source, w_all.at[shard, rows], w_send.at[sem if send is None else send], w_recv.at[sem], device
        )

    half_rows, later = part_rows // 2, HEAD - part_rows
    direct = [
        weights(w_hbm.at[quarter(turn(x, step))], head, quarter(turn(x, step)), side + min(step, 1), device)
        for step in range(RING) for side, device in ((0, y_next), (2, y_last))
    ]

    def passed(shard, which, begin, size, sem, device):
        rows = quarter(which, begin, size)
        return weights(w_all.at[shard, rows], shard, rows, sem, device)

    every_row = pl.ds(0, HEAD)
    ws = {
        4: passed(head_last, x, 0, half_rows, 4, y_next),
        5: passed(head_next, x, half_rows, half_rows, 5, y_last),
        6: passed(head_far, x, 0, part_rows, 6, x_next),
        7: passed(head_far, x, 0, part_rows, 7, x_last),
        8: passed(head_far, turn(x, -1), 0, half_rows, 8, x_next),
        9: passed(head_far, turn(x, 1), half_rows, half_rows, 9, x_last),
        10: weights(w_hbm, head, every_row, 10, pair),
        11: weights(w_all.at[head_last], head_last, every_row, 11, pair),
        12: weights(w_all.at[head_next], head_next, every_row, 12, pair),
        13: weights(w_all.at[head_far], head_far, every_row, 13, pair),
    }
    several = w_all.at[head, pl.ds(0, later)]
    for step in range(4):
        kv[step].start()
        qs[step].start()
    for copy in direct[:6]:
        copy.start()
    ws[10].start()
    announce(0, (z_next, z_last))

    ones = jnp.ones((BLK, HEAD), BF16)
    tokens = NB * BLK
    key_block = lax.broadcasted_iota(jnp.int32, (1, tokens), 1) // BLK

    def query_frame(slot):
        return x * RING + turn(z, -slot)

    def wide(slot, distance, k_ref, v_ref, valid):
        this = query_frame(slot)

        def pick(block):
            past = lax.rem(key_block + (NB - offset_ref[distance, block, this]), NB)
            inside = past < width_ref[distance, this]
            inside = inside | (key_block == jnp.where(distance == 0, block, NB))
            added = jnp.where(inside, 0.0, LOW)
            if valid is not None:
                added += jnp.where(valid, 0.0, LOW)
            return k_ref[...].reshape(tokens, HEAD), v_ref[...].reshape(tokens, HEAD), added

        return NB, pick

    def narrow(slot, distance, k_ref, v_ref, valid, count):
        this = query_frame(slot)

        def pick(block):
            offset = offset_ref[distance, block, this]
            chosen = [lax.rem(offset + step, NB) for step in range(count)]
            keys, values = [k_ref[index] for index in chosen], [v_ref[index] for index in chosen]
            if count > 1:
                keys, values = [jnp.concatenate(keys, axis=0)], [jnp.concatenate(values, axis=0)]
            return keys[0], values[0], None if valid is None else jnp.where(valid, 0.0, LOW)

        return count, pick

    def join(pieces):
        return pieces[0] if len(pieces) == 1 else jnp.concatenate(pieces, axis=0)

    def attend(slot, sources, first, blocks):
        count = sum(source[0] for source in sources)
        states, scores, values = [], [], []
        for block in blocks:
            picked = [source[1](block) for source in sources]
            full = lax.dot_general(
                q_all[slot, block], join([keys for keys, _, _ in picked]), (((1,), (1,)), ((), ())),
                preferred_element_type=F32,
            )
            parts = [full[:, step * BLK:(step + 1) * BLK] for step in range(count)]
            begin = 0
            for (size, _), (_, _, added) in zip(sources, picked):
                for step in range(size):
                    if added is not None:
                        more = added[:, step * BLK:(step + 1) * BLK] if added.ndim else added
                        parts[begin + step] += more
                begin += size
            scores.append(parts)
            values.append(join([rows for _, rows, _ in picked]))
        keeps, peaks = [], []
        for block, parts in zip(blocks, scores):
            peak = jnp.max(functools.reduce(jnp.maximum, parts), axis=1, keepdims=True)
            if not first:
                before = peak_ref[slot, block]
                peak = jnp.maximum(before, peak)
                keeps.append(jnp.exp2((before - peak) * EXPONENT))
            peaks.append(peak)
        updates = []
        for parts, peak, rows in zip(scores, peaks, values):
            weights = [jnp.exp2((part - peak) * EXPONENT).astype(BF16) for part in parts]
            weights = weights[0] if count == 1 else jnp.concatenate(weights, axis=1)
            extended = jnp.concatenate([rows, join([ones] * count)], axis=1)
            updates.append(jnp.dot(weights, extended, preferred_element_type=F32))
        for index, block in enumerate(blocks):
            mixed, total = updates[index][:, :HEAD], updates[index][:, HEAD:]
            if not first:
                mixed += mixed_ref[slot, block] * keeps[index]
                total += total_ref[slot, block] * keeps[index]
            states.append((jnp.broadcast_to(peaks[index], (BLK, HEAD)), total, mixed))
        return states

    def keep(slot, states, blocks):
        for block, (peak, total, mixed) in zip(blocks, states):
            peak_ref[slot, block] = peak
            total_ref[slot, block] = total
            mixed_ref[slot, block] = mixed

    def absorb(slot, sources, first, group):
        for begin in range(0, NB, group):
            blocks = range(begin, begin + group)
            keep(slot, attend(slot, sources, first, blocks), blocks)

    row = lax.broadcasted_iota(jnp.int32, (BLK, BLK), 0)
    lane = lax.broadcasted_iota(jnp.int32, (BLK, BLK), 1)
    small_row = lax.broadcasted_iota(jnp.int32, (8, BLK), 0)

    def pack(slot, states):
        for block, (peak, total, mixed) in enumerate(states):
            scaled = (mixed / total).astype(BF16)
            peak, total = (
                jnp.sum(jnp.where(row == lane, term, 0.0), axis=0, keepdims=True) for term in (peak, total)
            )
            level = peak * EXPONENT + jnp.log(total) * LOG2E
            first = level.astype(BF16).astype(F32)
            second = (level - first).astype(BF16).astype(F32)
            tile = jnp.where(
                small_row == 0, first,
                jnp.where(small_row == 1, second, jnp.where(small_row == 2, level - first - second, 0.0)),
            ).astype(BF16)
            for half in range(2):
                packed[slot, 2 * block + half, 0:ROWS, :] = scaled[half * ROWS:(half + 1) * ROWS]
                packed[slot, 2 * block + half, ROWS:PACKED, :] = tile

    def send(slot):
        def each(step, carry):
            receiver = lax.rem(2 * y + RING + step, HEADS)
            source, target = packed.at[slot, receiver], arrived.at[head, z]
            here = (slot == 0) & (receiver == head)

            @pl.when(here)
            def _():
                pltpu.make_async_copy(source, target, local_sem.at[4]).start()

            @pl.when(jnp.logical_not(here))
            def _():
                remote(
                    source, target, o_send.at[slot], o_recv.at[head], at(x, turn(z, -slot), receiver)
                ).start()

            return carry

        lax.fori_loop(0, HEADS, each, 0)

    every = range(NB)
    qs[0].wait_recv()
    qs[4].start()
    qs[1].wait_recv()
    qs[5].start()
    for copy in own[:3] + own[4:]:
        copy.wait()
    pl.semaphore_wait(ready.at[0], 2)
    announce(1, (y_next, y_last))

    def own_keys(step, carry):
        slot = step + lax.div(step, 2) - 2 * lax.div(step, 3)

        @pl.when(step == 1)
        def _():
            kv[0].wait_recv()
            kv[4].start()
            kv[1].wait_recv()
            kv[5].start()
            qs[2].wait_recv()
            qs[3].wait_recv()
            direct[0].wait_recv()
            ws[4].start()
            direct[1].wait_recv()
            ws[5].start()
            for copy in direct[6:]:
                copy.start()
            pl.semaphore_wait(ready.at[1], 2)
            announce(2, (y_next, y_last))

        @pl.when(step == 3)
        def _():
            qs[4].wait_recv()
            qs[5].wait_recv()
            pl.semaphore_wait(ready.at[2], 2)
            announce(3, (pair,))

        ahead = turn(z, -slot) - z
        distance = jnp.maximum(ahead, -ahead)

        @pl.when(distance <= 1)
        def _():
            absorb(slot, [wide(slot, distance, k_0, v_0, None)], True, 2)

        @pl.when(distance >= 2)
        def _():
            absorb(slot, [narrow(slot, distance, k_0, v_0, None, 2)], True, NB)

        return carry

    lax.fori_loop(0, RING, own_keys, 0)
    kv[2].wait_recv()
    kv[3].wait_recv()

    def near_keys(slot, carry):
        ahead = turn(z, -slot) - z
        distance = jnp.maximum(ahead, -ahead)
        last, next_ = (k_1, v_1, x >= 1), (k_3, v_3, x <= RING - 2)

        @pl.when(distance == 0)
        def _():
            absorb(slot, [narrow(slot, RING, *last, 1), narrow(slot, RING, *next_, 1)], False, NB)

        for sign, near, far in ((1, next_, last), (-1, last, next_)):

            @pl.when((ahead * sign >= 1) & (ahead * sign <= 2))
            def _():
                absorb(
                    slot,
                    [
                        narrow(slot, RING - distance, *near, 2),
                        narrow(slot, RING + distance, *far, 1),
                    ],
                    False, NB,
                )

            @pl.when(ahead * sign == 3)
            def _():
                absorb(slot, [wide(slot, 1, *near), narrow(slot, RADIUS, *far, 1)], False, 2)

        return carry

    lax.fori_loop(0, RING, near_keys, 0)

    ws[4].wait_recv()
    ws[5].wait_recv()
    ws[6].start()
    ws[7].start()
    pl.semaphore_wait(ready.at[3], 1)
    far_frame = turn(x, 2) * RING + z

    def far_keys(slot):
        this = query_frame(slot)
        distance = jnp.maximum(this - far_frame, far_frame - this)
        source = narrow(slot, jnp.minimum(distance, RADIUS), k_2, v_2, distance <= RADIUS, 1)
        return attend(slot, [source], False, every)

    pack(0, [(peak_ref[0, b], total_ref[0, b], mixed_ref[0, b]) for b in every])
    send(0)
    kv[4].wait_recv()
    kv[5].wait_recv()
    pack(2, far_keys(2))
    send(2)
    pack(3, far_keys(3))
    send(3)
    pack(1, far_keys(1))
    send(1)
    ws[6].wait_recv()
    ws[8].start()
    ws[7].wait_recv()
    ws[9].start()
    pltpu.make_async_copy(several, several, w_recv.at[1]).wait()
    ws[11].start()
    pltpu.make_async_copy(several, several, w_recv.at[3]).wait()
    ws[12].start()
    ws[8].wait_recv()
    ws[9].wait_recv()
    ws[13].start()

    column = lax.broadcasted_iota(jnp.int32, (ROWS, HEAD), 1)
    here = lax.broadcasted_iota(jnp.int32, (ROWS, HEAD), 0) + core * ROWS

    def merge(other):
        levels = []
        for part in range(RING):
            tile = arrived[other, part, ROWS:PACKED, :].astype(F32)
            levels.append(jnp.sum(tile, axis=0, keepdims=True))
        peak = functools.reduce(jnp.maximum, levels)
        shares = [jnp.exp2(level - peak) for level in levels]
        whole = functools.reduce(jnp.add, shares)
        merged = jnp.zeros((ROWS, HEAD), F32)
        for part in range(RING):
            share = jnp.broadcast_to(shares[part] / whole, (ROWS, HEAD))
            share = jnp.sum(jnp.where(column == here, share, 0.0), axis=1, keepdims=True)
            merged += arrived[other, part, 0:ROWS, :].astype(F32) * share
        return merged.astype(BF16)

    pltpu.make_async_copy(packed.at[0, head], arrived.at[head, z], local_sem.at[4]).wait()
    own[3].wait()
    for step in range(10, 13):
        ws[step].wait_recv()

    columns, tile = w_all.shape[2], 512
    for index, step in enumerate((0, -1, 1, 2)):
        chip = turn(y, step)
        if step == 2:
            ws[13].wait_recv()
        for side in range(2):
            other = chip * 2 + side

            @pl.when(other == head)
            def _():
                three = arrived.at[other, pl.ds(0, RING - 1)]
                pltpu.make_async_copy(three, three, o_recv.at[other]).wait()

            @pl.when(other != head)
            def _():
                pltpu.make_async_copy(arrived.at[other], arrived.at[other], o_recv.at[other]).wait()

        left = jnp.concatenate([merge(chip * 2), merge(chip * 2 + 1)], axis=1)
        for start in range(0, columns, tile):
            weight = w_all[pl.ds(chip * 2, 2), :, start:start + tile].reshape(2 * HEAD, tile)
            term = jnp.dot(left, weight, preferred_element_type=F32)
            if index > 0:
                term += sums[:, start:start + tile]
            if index < RING - 1:
                sums[:, start:start + tile] = term
            else:
                out_ref[:, start:start + tile] = term

    for copy in kv + qs + direct[:2] + list(ws.values()):
        copy.wait_send()
    for sem in (1, 3):
        pltpu.make_async_copy(several, several, w_send.at[sem]).wait()
    seven = packed.at[0, pl.ds(0, HEADS - 1)]
    pltpu.make_async_copy(seven, seven, o_send.at[0]).wait()
    for slot in range(1, RING):
        pltpu.make_async_copy(packed.at[slot], packed.at[slot], o_send.at[slot]).wait()


def on_device(queries, keys, values, band_width, band_offset, out_weight):
    width = out_weight.shape[1]
    queries, keys, values = (array.reshape(NB, BLK, HEAD) for array in (queries, keys, values))
    band_width, band_offset = band_width.T, band_offset.transpose(1, 2, 0)
    band_width, band_offset, queries, keys, values, out_weight = (
        pltpu.with_memory_space_constraint(array, pltpu.HBM)
        for array in (band_width, band_offset, queries, keys, values, out_weight)
    )
    block = pltpu.VMEM((NB, BLK, HEAD), BF16)
    state = pltpu.VMEM((RING, NB, BLK, HEAD), F32)
    dma = pltpu.SemaphoreType.DMA
    anywhere = pl.BlockSpec(memory_space=pltpu.HBM)
    return pl.pallas_call(
        kernel,
        out_shape=jax.ShapeDtypeStruct((ROWS, width), F32),
        in_specs=[anywhere] * 6,
        out_specs=pl.BlockSpec(memory_space=pltpu.VMEM),
        scratch_shapes=[pltpu.SMEM(band_width.shape, jnp.int32), pltpu.SMEM(band_offset.shape, jnp.int32)]
        + [block] * 8
        + [
            pltpu.VMEM((RING, NB, BLK, HEAD), BF16),
            pltpu.VMEM((HEADS, HEAD, width), BF16),
            state, state, state,
            pltpu.VMEM((RING, HEADS, PACKED, HEAD), BF16),
            pltpu.VMEM((HEADS, RING, PACKED, HEAD), BF16),
            pltpu.VMEM((ROWS, width), F32),
            dma((7,)), dma((6,)), dma((6,)), dma((6,)), dma((6,)), dma((14,)), dma((14,)),
            dma((RING,)), dma((HEADS,)), pltpu.SemaphoreType.REGULAR((4,)),
        ],
        compiler_params=pltpu.CompilerParams(
            collective_id=0, has_side_effects=True, vmem_limit_bytes=52 * 1024 * 1024
        ),
    )(band_width, band_offset, queries, keys, values, out_weight).astype(BF16)


def solution(mesh):
    placed = (P("frame", "head"), P("frame", "head"), P("frame", "head"), P(), P(), P("head", None))
    return jax.shard_map(
        on_device, mesh=mesh, in_specs=placed, out_specs=P(("frame", "head"), None), check_vma=False
    )
```

```python
import functools
import math

import jax
import jax.numpy as jnp
from jax import lax
from jax.experimental import pallas as pl
from jax.experimental.pallas import tpu as pltpu
from jax.sharding import PartitionSpec as P

RING = 4
HEADS = 8
HEAD = 128
BLK = 128
NB = 4
RADIUS = 7
ROWS = 64
HALF = NB // 2
PACKED = ROWS + 8
LOG2E = math.log2(math.e)
EXPONENT = LOG2E / math.sqrt(HEAD)
LOW = -1e30
MESH = pl.DeviceIdType.MESH
BF16, F32 = jnp.bfloat16, jnp.float32


def turn(value, steps):
    return lax.rem(value + (RING + steps), RING)


def kernel(
    width_hbm, offset_hbm, q_hbm, k_hbm, v_hbm, w_hbm, out_ref,
    width_ref, offset_ref, k_0, k_1, k_2, k_3, v_0, v_1, v_2, v_3, q_all, w_all,
    peak_ref, total_ref, mixed_ref, packed, arrived, sums,
    local_sem, kv_send, kv_recv, q_send, q_recv, w_send, w_recv, o_send, o_recv, ready,
):
    frame, head = lax.axis_index("frame"), lax.axis_index("head")
    x, z = lax.div(frame, RING), lax.rem(frame, RING)
    y, core = lax.div(head, 2), lax.rem(head, 2)

    def at(x, z, head):
        return (x * RING + z, head)

    x_next, x_last = at(turn(x, 1), z, head), at(turn(x, -1), z, head)
    z_next, z_last = at(x, turn(z, 1), head), at(x, turn(z, -1), head)
    head_next, head_last = turn(y, 1) * 2 + core, turn(y, -1) * 2 + core
    head_far, head_pair = turn(y, 2) * 2 + core, y * 2 + 1 - core
    y_next, y_last, pair = at(x, z, head_next), at(x, z, head_last), at(x, z, head_pair)
    def remote(source, target, send, recv, device):
        return pltpu.make_async_remote_copy(
            src_ref=source, dst_ref=target, send_sem=send, recv_sem=recv,
            device_id=device, device_id_type=MESH,
        )

    barrier = pltpu.get_barrier_semaphore()
    greeted = [x_next, x_last, z_next, z_last, y_next, y_last, pair]
    for device in greeted:
        pl.semaphore_signal(barrier, inc=1, device_id=device, device_id_type=MESH)

    def announce(turn_, devices):
        for device in devices:
            pl.semaphore_signal(ready.at[turn_], inc=1, device_id=device, device_id_type=MESH)

    own = [
        pltpu.make_async_copy(q_hbm, q_all.at[0], local_sem.at[0]),
        pltpu.make_async_copy(k_hbm, k_0, local_sem.at[1]),
        pltpu.make_async_copy(v_hbm, v_0, local_sem.at[2]),
        pltpu.make_async_copy(w_hbm, w_all.at[head], local_sem.at[3]),
        pltpu.make_async_copy(width_hbm, width_ref, local_sem.at[5]),
        pltpu.make_async_copy(offset_hbm, offset_ref, local_sem.at[6]),
    ]
    for copy in own:
        copy.start()
    pl.semaphore_wait(barrier, len(greeted))

    kv = [
        remote(k_hbm, k_1, kv_send.at[0], kv_recv.at[0], x_next),
        remote(v_hbm, v_3, kv_send.at[1], kv_recv.at[1], x_last),
        remote(v_hbm, v_1, kv_send.at[2], kv_recv.at[2], x_next),
        remote(k_hbm, k_3, kv_send.at[3], kv_recv.at[3], x_last),
        remote(k_1, k_2, kv_send.at[4], kv_recv.at[4], x_next),
        remote(v_3, v_2, kv_send.at[5], kv_recv.at[5], x_last),
    ]
    low, high = pl.ds(0, HALF), pl.ds(HALF, HALF)
    qs = [
        remote(q_hbm.at[low], q_all.at[1, low], q_send.at[0], q_recv.at[0], z_next),
        remote(q_hbm.at[high], q_all.at[3, high], q_send.at[1], q_recv.at[1], z_last),
        remote(q_hbm.at[high], q_all.at[1, high], q_send.at[2], q_recv.at[2], z_next),
        remote(q_hbm.at[low], q_all.at[3, low], q_send.at[3], q_recv.at[3], z_last),
        remote(q_all.at[1, low], q_all.at[2, low], q_send.at[4], q_recv.at[4], z_next),
        remote(q_all.at[3, high], q_all.at[2, high], q_send.at[5], q_recv.at[5], z_last),
    ]
    part_rows = HEAD // RING

    def quarter(which, begin=0, size=part_rows):
        return pl.ds(pl.multiple_of(which * part_rows + begin, part_rows // 2), size)

    def weights(source, shard, rows, sem, device, send=None):
        return remote(
            source, w_all.at[shard, rows], w_send.at[sem if send is None else send], w_recv.at[sem], device
        )

    half_rows, later = part_rows // 2, HEAD - part_rows
    direct = [
        weights(w_hbm.at[quarter(turn(x, step))], head, quarter(turn(x, step)), side + min(step, 1), device)
        for step in range(RING) for side, device in ((0, y_next), (2, y_last))
    ]

    def passed(shard, which, begin, size, sem, device):
        rows = quarter(which, begin, size)
        return weights(w_all.at[shard, rows], shard, rows, sem, device)

    every_row = pl.ds(0, HEAD)
    ws = {
        4: passed(head_last, x, 0, half_rows, 4, y_next),
        5: passed(head_next, x, half_rows, half_rows, 5, y_last),
        6: passed(head_far, x, 0, part_rows, 6, x_next),
        7: passed(head_far, x, 0, part_rows, 7, x_last),
        8: passed(head_far, turn(x, -1), 0, half_rows, 8, x_next),
        9: passed(head_far, turn(x, 1), half_rows, half_rows, 9, x_last),
        10: weights(w_hbm, head, every_row, 10, pair),
        11: weights(w_all.at[head_last], head_last, every_row, 11, pair),
        12: weights(w_all.at[head_next], head_next, every_row, 12, pair),
        13: weights(w_all.at[head_far], head_far, every_row, 13, pair),
    }
    several = w_all.at[head, pl.ds(0, later)]
    for step in range(4):
        kv[step].start()
        qs[step].start()
    for copy in direct[:6]:
        copy.start()
    ws[10].start()
    announce(0, (z_next, z_last))

    ones = jnp.ones((BLK, HEAD), BF16)
    tokens = NB * BLK
    key_block = lax.broadcasted_iota(jnp.int32, (1, tokens), 1) // BLK

    def query_frame(slot):
        return x * RING + turn(z, -slot)

    def wide(slot, distance, k_ref, v_ref, valid):
        this = query_frame(slot)

        def pick(block):
            past = lax.rem(key_block + (NB - offset_ref[distance, block, this]), NB)
            inside = past < width_ref[distance, this]
            inside = inside | (key_block == jnp.where(distance == 0, block, NB))
            added = jnp.where(inside, 0.0, LOW)
            if valid is not None:
                added += jnp.where(valid, 0.0, LOW)
            return k_ref[...].reshape(tokens, HEAD), v_ref[...].reshape(tokens, HEAD), added

        return NB, pick

    def narrow(slot, distance, k_ref, v_ref, valid, count):
        this = query_frame(slot)

        def pick(block):
            offset = offset_ref[distance, block, this]
            chosen = [lax.rem(offset + step, NB) for step in range(count)]
            keys, values = [k_ref[index] for index in chosen], [v_ref[index] for index in chosen]
            if count > 1:
                keys, values = [jnp.concatenate(keys, axis=0)], [jnp.concatenate(values, axis=0)]
            return keys[0], values[0], None if valid is None else jnp.where(valid, 0.0, LOW)

        return count, pick

    def join(pieces):
        return pieces[0] if len(pieces) == 1 else jnp.concatenate(pieces, axis=0)

    def attend(slot, sources, first, blocks):
        count = sum(source[0] for source in sources)
        states, scores, values = [], [], []
        for block in blocks:
            picked = [source[1](block) for source in sources]
            full = lax.dot_general(
                q_all[slot, block], join([keys for keys, _, _ in picked]), (((1,), (1,)), ((), ())),
                preferred_element_type=F32,
            )
            parts = [full[:, step * BLK:(step + 1) * BLK] for step in range(count)]
            begin = 0
            for (size, _), (_, _, added) in zip(sources, picked):
                for step in range(size):
                    if added is not None:
                        more = added[:, step * BLK:(step + 1) * BLK] if added.ndim else added
                        parts[begin + step] += more
                begin += size
            scores.append(parts)
            values.append(join([rows for _, rows, _ in picked]))
        keeps, peaks = [], []
        for block, parts in zip(blocks, scores):
            peak = jnp.max(functools.reduce(jnp.maximum, parts), axis=1, keepdims=True)
            if not first:
                before = peak_ref[slot, block]
                peak = jnp.maximum(before, peak)
                keeps.append(jnp.exp2((before - peak) * EXPONENT))
            peaks.append(peak)
        updates = []
        for parts, peak, rows in zip(scores, peaks, values):
            weights = [jnp.exp2((part - peak) * EXPONENT).astype(BF16) for part in parts]
            weights = weights[0] if count == 1 else jnp.concatenate(weights, axis=1)
            extended = jnp.concatenate([rows, join([ones] * count)], axis=1)
            updates.append(jnp.dot(weights, extended, preferred_element_type=F32))
        for index, block in enumerate(blocks):
            mixed, total = updates[index][:, :HEAD], updates[index][:, HEAD:]
            if not first:
                mixed += mixed_ref[slot, block] * keeps[index]
                total += total_ref[slot, block] * keeps[index]
            states.append((jnp.broadcast_to(peaks[index], (BLK, HEAD)), total, mixed))
        return states

    def keep(slot, states, blocks):
        for block, (peak, total, mixed) in zip(blocks, states):
            peak_ref[slot, block] = peak
            total_ref[slot, block] = total
            mixed_ref[slot, block] = mixed

    def absorb(slot, sources, first, group):
        for begin in range(0, NB, group):
            blocks = range(begin, begin + group)
            keep(slot, attend(slot, sources, first, blocks), blocks)

    row = lax.broadcasted_iota(jnp.int32, (BLK, BLK), 0)
    lane = lax.broadcasted_iota(jnp.int32, (BLK, BLK), 1)
    small_row = lax.broadcasted_iota(jnp.int32, (8, BLK), 0)

    def pack(slot, states):
        for block, (peak, total, mixed) in enumerate(states):
            scaled = (mixed / total).astype(BF16)
            level = peak * EXPONENT + jnp.log(total) * LOG2E
            level = jnp.sum(jnp.where(row == lane, level, 0.0), axis=0, keepdims=True)
            first = level.astype(BF16).astype(F32)
            second = (level - first).astype(BF16).astype(F32)
            tile = jnp.where(
                small_row == 0, first,
                jnp.where(small_row == 1, second, jnp.where(small_row == 2, level - first - second, 0.0)),
            ).astype(BF16)
            for half in range(2):
                packed[slot, 2 * block + half, 0:ROWS, :] = scaled[half * ROWS:(half + 1) * ROWS]
                packed[slot, 2 * block + half, ROWS:PACKED, :] = tile

    def send(slot):
        def each(step, carry):
            receiver = lax.rem(2 * y + RING + step, HEADS)
            source, target = packed.at[slot, receiver], arrived.at[head, z]
            here = (slot == 0) & (receiver == head)

            @pl.when(here)
            def _():
                pltpu.make_async_copy(source, target, local_sem.at[4]).start()

            @pl.when(jnp.logical_not(here))
            def _():
                remote(
                    source, target, o_send.at[slot], o_recv.at[head], at(x, turn(z, -slot), receiver)
                ).start()

            return carry

        lax.fori_loop(0, HEADS, each, 0)

    every = range(NB)
    qs[0].wait_recv()
    qs[4].start()
    qs[1].wait_recv()
    qs[5].start()
    for copy in own[:3] + own[4:]:
        copy.wait()
    pl.semaphore_wait(ready.at[0], 2)
    announce(1, (y_next, y_last))

    def own_keys(step, carry):
        slot = step + lax.div(step, 2) - 2 * lax.div(step, 3)

        @pl.when(step == 1)
        def _():
            kv[0].wait_recv()
            kv[4].start()
            kv[1].wait_recv()
            kv[5].start()
            qs[2].wait_recv()
            qs[3].wait_recv()
            direct[0].wait_recv()
            ws[4].start()
            direct[1].wait_recv()
            ws[5].start()
            for copy in direct[6:]:
                copy.start()
            pl.semaphore_wait(ready.at[1], 2)
            announce(2, (y_next, y_last))

        @pl.when(step == 3)
        def _():
            qs[4].wait_recv()
            qs[5].wait_recv()
            pl.semaphore_wait(ready.at[2], 2)
            announce(3, (pair,))

        ahead = turn(z, -slot) - z
        distance = jnp.maximum(ahead, -ahead)

        @pl.when(distance <= 1)
        def _():
            absorb(slot, [wide(slot, distance, k_0, v_0, None)], True, 2)

        @pl.when(distance >= 2)
        def _():
            absorb(slot, [narrow(slot, distance, k_0, v_0, None, 2)], True, NB)

        return carry

    lax.fori_loop(0, RING, own_keys, 0)
    kv[2].wait_recv()
    kv[3].wait_recv()

    def near_keys(slot, carry):
        ahead = turn(z, -slot) - z
        distance = jnp.maximum(ahead, -ahead)
        last, next_ = (k_1, v_1, x >= 1), (k_3, v_3, x <= RING - 2)

        @pl.when(distance == 0)
        def _():
            absorb(slot, [narrow(slot, RING, *last, 1), narrow(slot, RING, *next_, 1)], False, NB)

        for sign, near, far in ((1, next_, last), (-1, last, next_)):

            @pl.when((ahead * sign >= 1) & (ahead * sign <= 2))
            def _():
                absorb(
                    slot,
                    [
                        narrow(slot, RING - distance, *near, 2),
                        narrow(slot, RING + distance, *far, 1),
                    ],
                    False, NB,
                )

            @pl.when(ahead * sign == 3)
            def _():
                absorb(slot, [wide(slot, 1, *near), narrow(slot, RADIUS, *far, 1)], False, 2)

        return carry

    lax.fori_loop(0, RING, near_keys, 0)

    pl.semaphore_wait(ready.at[3], 1)
    far_frame = turn(x, 2) * RING + z

    def far_keys(slot):
        this = query_frame(slot)
        distance = jnp.maximum(this - far_frame, far_frame - this)
        source = narrow(slot, jnp.minimum(distance, RADIUS), k_2, v_2, distance <= RADIUS, 1)
        return attend(slot, [source], False, every)

    pack(0, [(peak_ref[0, b], total_ref[0, b], mixed_ref[0, b]) for b in every])
    send(0)
    kv[4].wait_recv()
    kv[5].wait_recv()
    ws[4].wait_recv()
    ws[5].wait_recv()
    ws[6].start()
    ws[7].start()
    pack(2, far_keys(2))
    send(2)
    states = far_keys(3), far_keys(1)
    pack(3, states[0])
    pack(1, states[1])
    send(3)
    send(1)
    ws[6].wait_recv()
    ws[8].start()
    ws[7].wait_recv()
    ws[9].start()
    pltpu.make_async_copy(several, several, w_recv.at[1]).wait()
    ws[11].start()
    pltpu.make_async_copy(several, several, w_recv.at[3]).wait()
    ws[12].start()
    ws[8].wait_recv()
    ws[9].wait_recv()
    ws[13].start()

    column = lax.broadcasted_iota(jnp.int32, (ROWS, HEAD), 1)
    here = lax.broadcasted_iota(jnp.int32, (ROWS, HEAD), 0) + core * ROWS

    def merge(other):
        levels = []
        for part in range(RING):
            tile = arrived[other, part, ROWS:PACKED, :].astype(F32)
            levels.append(jnp.sum(tile, axis=0, keepdims=True))
        peak = functools.reduce(jnp.maximum, levels)
        shares = [jnp.exp2(level - peak) for level in levels]
        whole = functools.reduce(jnp.add, shares)
        merged = jnp.zeros((ROWS, HEAD), F32)
        for part in range(RING):
            share = jnp.broadcast_to(shares[part] / whole, (ROWS, HEAD))
            share = jnp.sum(jnp.where(column == here, share, 0.0), axis=1, keepdims=True)
            merged += arrived[other, part, 0:ROWS, :].astype(F32) * share
        return merged.astype(BF16)

    pltpu.make_async_copy(packed.at[0, head], arrived.at[head, z], local_sem.at[4]).wait()
    own[3].wait()
    for step in range(10, 13):
        ws[step].wait_recv()

    columns, tile = w_all.shape[2], 512
    for index, step in enumerate((0, -1, 1, 2)):
        chip = turn(y, step)
        if step == 2:
            ws[13].wait_recv()
        for side in range(2):
            other = chip * 2 + side

            @pl.when(other == head)
            def _():
                three = arrived.at[other, pl.ds(0, RING - 1)]
                pltpu.make_async_copy(three, three, o_recv.at[other]).wait()

            @pl.when(other != head)
            def _():
                pltpu.make_async_copy(arrived.at[other], arrived.at[other], o_recv.at[other]).wait()

        left = jnp.concatenate([merge(chip * 2), merge(chip * 2 + 1)], axis=1)
        for start in range(0, columns, tile):
            weight = w_all[pl.ds(chip * 2, 2), :, start:start + tile].reshape(2 * HEAD, tile)
            term = jnp.dot(left, weight, preferred_element_type=F32)
            if index > 0:
                term += sums[:, start:start + tile]
            if index < RING - 1:
                sums[:, start:start + tile] = term
            else:
                out_ref[:, start:start + tile] = term

    for copy in kv + qs + direct[:2] + list(ws.values()):
        copy.wait_send()
    for sem in (1, 3):
        pltpu.make_async_copy(several, several, w_send.at[sem]).wait()
    seven = packed.at[0, pl.ds(0, HEADS - 1)]
    pltpu.make_async_copy(seven, seven, o_send.at[0]).wait()
    for slot in range(1, RING):
        pltpu.make_async_copy(packed.at[slot], packed.at[slot], o_send.at[slot]).wait()


def on_device(queries, keys, values, band_width, band_offset, out_weight):
    width = out_weight.shape[1]
    queries, keys, values = (array.reshape(NB, BLK, HEAD) for array in (queries, keys, values))
    band_width, band_offset = band_width.T, band_offset.transpose(1, 2, 0)
    band_width, band_offset, queries, keys, values, out_weight = (
        pltpu.with_memory_space_constraint(array, pltpu.HBM)
        for array in (band_width, band_offset, queries, keys, values, out_weight)
    )
    block = pltpu.VMEM((NB, BLK, HEAD), BF16)
    state = pltpu.VMEM((RING, NB, BLK, HEAD), F32)
    dma = pltpu.SemaphoreType.DMA
    anywhere = pl.BlockSpec(memory_space=pltpu.HBM)
    return pl.pallas_call(
        kernel,
        out_shape=jax.ShapeDtypeStruct((ROWS, width), F32),
        in_specs=[anywhere] * 6,
        out_specs=pl.BlockSpec(memory_space=pltpu.VMEM),
        scratch_shapes=[pltpu.SMEM(band_width.shape, jnp.int32), pltpu.SMEM(band_offset.shape, jnp.int32)]
        + [block] * 8
        + [
            pltpu.VMEM((RING, NB, BLK, HEAD), BF16),
            pltpu.VMEM((HEADS, HEAD, width), BF16),
            state, state, state,
            pltpu.VMEM((RING, HEADS, PACKED, HEAD), BF16),
            pltpu.VMEM((HEADS, RING, PACKED, HEAD), BF16),
            pltpu.VMEM((ROWS, width), F32),
            dma((7,)), dma((6,)), dma((6,)), dma((6,)), dma((6,)), dma((14,)), dma((14,)),
            dma((RING,)), dma((HEADS,)), pltpu.SemaphoreType.REGULAR((4,)),
        ],
        compiler_params=pltpu.CompilerParams(
            collective_id=0, has_side_effects=True, vmem_limit_bytes=52 * 1024 * 1024
        ),
    )(band_width, band_offset, queries, keys, values, out_weight).astype(BF16)


def solution(mesh):
    placed = (P("frame", "head"), P("frame", "head"), P("frame", "head"), P(), P(), P("head", None))
    return jax.shard_map(
        on_device, mesh=mesh, in_specs=placed, out_specs=P(("frame", "head"), None), check_vma=False
    )
```
